32 devices in a mesh: angle: 8 (over z, x), row: 4 (over y, core).
Axes of the slice: x: 2, y: 2, z: 4, core: 2. Of those that a mesh axis runs over, the one named last changes fastest.
Arguments:
- raw_frames: bfloat16 [8, 8, 32, 2048], P('angle', None, 'row'), may hold values from 0.5 to 1.5
- step_index: int32 [8, 8], P('angle'), may hold values from 0 to 7, each once within a row
- partner: int32 [8], replicated, may hold values from 0 to 7, as said below
- flat_field: bfloat16 [2, 32, 2048], P(None, ('row', 'angle')), may hold values from -4 to 4
Outputs:
- filtered: bfloat16 [8, 32, 2048], P(None, ('row', 'angle'))
The draws below stay inside these ranges and needn't reach their ends.
Inputs may be any that keep to these rules, and one draw needn't show every extreme that they name: partner[partner[a]] = a, and every angle of the first half of the 8 angles is paired with one of the second half. `step_index`: each angle's row names every phase step once.
All inputs are finite; a program needn't handle non-finite values.
Results may differ from the reference program's by a relative error of at most 0.0078.
Values may be sent and summed in bfloat16 or wider, within the bound.
A program may use at most 128 MiB of HBM per device.

```python
import math
import jax
import jax.numpy as jnp
from jax import lax

DET = 2048
STEPS = 8
PAD = 4096
ANGLES = 8
ROWS = 32


def draw_partner(key, part):
    half = ANGLES // 2
    order = jax.random.permutation(jax.random.fold_in(key, 17), half).astype(jnp.int32)
    inverse = jnp.argsort(order).astype(jnp.int32)
    return jnp.concatenate([order + half, inverse]).astype(jnp.int32)


def level_of(rng, shape, shards, least, largest):
    gain = 1.0
    for axis_at, blocks in shards:
        draws = jax.random.uniform(jax.random.fold_in(jax.random.fold_in(rng, 6), axis_at), (blocks,), jnp.float32, least / len(shards), largest / len(shards))
        gain = gain * jnp.repeat(jnp.exp(draws), shape[axis_at] // blocks).reshape((-1,) + (1,) * (len(shape) - 1 - axis_at))
    return gain


def bell_draw(key, extent, deviation, most, cuts=(), kind=jnp.bfloat16):
    array = deviation * jax.random.normal(key, extent, jnp.float32)
    if cuts:
        array = array * level_of(key, extent, cuts, -0.22, 0.18)
    return jnp.clip(array, -most, most).astype(kind)


def setup_inputs(seed: int = 0) -> dict:
    splits = jax.random.split(jax.random.key(seed), 5)
    return {
        "raw_frames": jnp.clip(0.5 + 1.0 * jax.random.uniform(splits[0], (ANGLES, STEPS, ROWS, DET), jnp.float32) ** level_of(splits[0], (ANGLES, STEPS, ROWS, DET), ((0, 8), (2, 4)), -0.2, 0.2), 0.5, 1.5).astype(jnp.bfloat16),
        "step_index": jax.vmap(lambda own: jax.random.permutation(own, STEPS))(jax.random.split(splits[1], ANGLES)).reshape((ANGLES, STEPS)).astype(jnp.int32),
        "partner": draw_partner(jax.random.fold_in(splits[4], 71), 0),
        "flat_field": bell_draw(splits[3], (2, ROWS, DET), 1.0, 4.0, ((1, 32),)),
    }


two_pi = 2.0 * math.pi


def smooth_rows(field):
    padded = jnp.pad(field, ((0, 0), (1, 1), (0, 0)))
    return (0.25 * padded[:, :-2] + 0.5 * padded[:, 1:-1] + 0.25 * padded[:, 2:]).astype(jnp.bfloat16)


def reference(raw_frames, step_index, partner, flat_field):
    phase = step_index.astype(jnp.float32) * (two_pi / STEPS)
    weight_cos = jnp.cos(phase)
    weight_sin = jnp.sin(phase)
    corr_cos = jnp.zeros((ANGLES, ROWS, DET), jnp.float32)
    corr_sin = jnp.zeros((ANGLES, ROWS, DET), jnp.float32)
    corr_mean = jnp.zeros((ANGLES, ROWS, DET), jnp.float32)
    for step in range(STEPS):
        frame = raw_frames[:, step].astype(jnp.float32)
        corr_cos = corr_cos + frame * weight_cos[:, step][:, None, None]
        corr_sin = corr_sin + frame * weight_sin[:, step][:, None, None]
        corr_mean = corr_mean + frame
    smooth_cos = smooth_rows(corr_cos).astype(jnp.float32)
    smooth_sin = smooth_rows(corr_sin).astype(jnp.float32)
    smooth_mean = smooth_rows(corr_mean).astype(jnp.float32)
    flat = flat_field.astype(jnp.float32)
    dpc = (STEPS * (smooth_sin * flat[0][None] - smooth_cos * flat[1][None]) / smooth_mean).astype(jnp.bfloat16)
    mirror = jnp.take(dpc, partner.astype(jnp.int32), axis=0)[:, :, ::-1]
    combined = jnp.concatenate([-mirror, dpc], axis=2)
    column = lax.broadcasted_iota(jnp.int32, (PAD, DET), 0)
    freq = lax.broadcasted_iota(jnp.int32, (PAD, DET), 1)
    theta = ((column * freq) % PAD).astype(jnp.float32) * (two_pi / PAD)
    cos_table = jnp.cos(theta).astype(jnp.bfloat16)
    sin_table = jnp.sin(theta).astype(jnp.bfloat16)
    cos_own = cos_table[DET:]
    sin_own = sin_table[DET:]
    by_row = jnp.transpose(combined, (1, 0, 2))

    def filter_one(rows):
        spec_cos = jnp.dot(rows, cos_table, preferred_element_type=jnp.float32).astype(jnp.bfloat16)
        spec_sin = jnp.dot(rows, sin_table, preferred_element_type=jnp.float32).astype(jnp.bfloat16)
        first = jnp.dot(spec_cos, sin_own.T, preferred_element_type=jnp.float32)
        second = jnp.dot(spec_sin, cos_own.T, preferred_element_type=jnp.float32)
        return ((first - second) * (2.0 / PAD)).astype(jnp.bfloat16)

    filtered = lax.map(filter_one, by_row)
    return jnp.transpose(filtered, (1, 0, 2))
```

```python
import math

import jax
import jax.numpy as jnp
import ml_dtypes
import numpy as np
from jax import lax
from jax.experimental import pallas as pl
from jax.experimental.pallas import tpu as pltpu
from jax.sharding import PartitionSpec as P

WIDTH = 256
LANES = 128
TILE = 8
PIECES = 2


def circulant_blocks(padlen):
    count = padlen // WIDTH
    n = np.arange(padlen, dtype=np.float64)
    odd = np.arange(padlen) % 2 == 1
    taps = np.where(odd, (2.0 / padlen) / np.tan(np.pi * np.where(odd, n, 1.0) / padlen), 0.0)
    m = np.arange(count)[:, None, None]
    p = np.arange(WIDTH)[None, :, None]
    q = np.arange(WIDTH)[None, None, :]
    return taps[(WIDTH * m + q - p) % padlen].astype(ml_dtypes.bfloat16)


def loop(start, stop, body):
    if isinstance(start, int) and isinstance(stop, int) and stop - start <= 8:
        for i in range(start, stop):
            body(i)
    else:
        lax.fori_loop(start, stop, lambda i, _: body(i), None)


def aligned(value, step):
    return value if isinstance(value, int) else pl.multiple_of(value, step)


def kernel(
    angles, blocks_row, raw_hbm, step_hbm, partner_hbm, flat_hbm, table_hbm, out_ref,
    raw_first, raw_second, table, step_ref, partner_ref, flat_ref, flat_rows, corr, halo, partial, edge, both, smooth, recv, natural, mirrored, ring,
    local_sem, halo_send, halo_recv, send_sem, recv_sem, ready,
):
    raw = (raw_first, raw_second)
    steps, rows, _ = raw_first.shape
    det = flat_ref.shape[1]
    chunks = det // LANES
    per = chunks // PIECES
    own = det // WIDTH
    last = angles - 1
    me = lax.axis_index("angle")
    row = lax.axis_index("row")
    after = lax.rem(row + 1, blocks_row)
    before = lax.rem(row + blocks_row - 1, blocks_row)
    has_before = row > 0
    has_after = row < blocks_row - 1
    odd = lax.rem(row, 2) == 1
    even = jnp.logical_not(odd)
    cross_before = has_before & even
    cross_after = has_after & odd
    first_row = (me == 0) & cross_before
    last_row = (me == last) & cross_after
    merged = first_row | last_row

    barrier = pltpu.get_barrier_semaphore()

    step_copy = pltpu.make_async_copy(step_hbm, step_ref, local_sem.at[0])
    step_copy.start()

    def raw_copy(p):
        lanes = pl.ds(p * per * LANES, per * LANES)
        return pltpu.make_async_copy(raw_hbm.at[0, :, :, lanes], raw[p], local_sem.at[4 + p])

    for p in range(PIECES):
        raw_copy(p).start()

    def greet(a):
        pl.semaphore_signal(barrier, inc=1, device_id={"angle": a})

    loop(me + 1, angles, greet)

    @pl.when(even)
    def _():
        pl.semaphore_signal(barrier, inc=1, device_id={"row": after})

    @pl.when(odd)
    def _():
        pl.semaphore_signal(barrier, inc=1, device_id={"row": before})

    @pl.when(first_row)
    def _():
        loop(0, angles, lambda a: pl.semaphore_signal(
            barrier, inc=1, device_id={"angle": a, "row": before}
        ))

    @pl.when(last_row)
    def _():
        loop(0, angles, lambda a: pl.semaphore_signal(
            barrier, inc=1, device_id={"angle": a, "row": after}
        ))

    table_copy = pltpu.make_async_copy(table_hbm, table, local_sem.at[1])
    table_copy.start()
    partner_copy = pltpu.make_async_copy(partner_hbm, partner_ref, local_sem.at[2])
    partner_copy.start()
    flat_copy = pltpu.make_async_copy(flat_hbm, flat_ref, local_sem.at[3])
    flat_copy.start()
    step_copy.wait()

    named = [step_ref[0, k] for k in range(steps)]
    frame_of = []
    for i in range(steps):
        at = jnp.int32(0)
        for k in range(1, steps):
            at = jnp.where(named[k] == i, jnp.int32(k), at)
        frame_of.append(at)
    assert steps == 8
    half_root = float(np.float32(math.sqrt(0.5)))

    def correlate(p, g):
        at = aligned(g * TILE, TILE)
        sums = [[], [], []]
        for c in range(per):
            f = [
                raw[p][frame_of[i], pl.ds(at, TILE), c * LANES : (c + 1) * LANES].astype(jnp.float32)
                for i in range(steps)
            ]
            less = [f[i] - f[i + 4] for i in range(4)]
            more = [f[i] + f[i + 4] for i in range(4)]
            sums[0].append(less[0] + (less[1] - less[3]) * half_root)
            sums[1].append(less[2] + (less[1] + less[3]) * half_root)
            sums[2].append((more[0] + more[2]) + (more[1] + more[3]))
        for q in range(3):
            turned = jnp.swapaxes(jnp.stack(sums[q]), 0, 1)
            for j in range(TILE):
                corr[q, pl.ds(aligned((at + j) * chunks + p * per, TILE), per), :] = turned[j]

    def line(p, q, i):
        return corr[q, pl.ds(aligned(i * chunks + p * per, TILE), per), :]

    def part_of(p):
        return slice(p * per, (p + 1) * per)

    def ratios(p, i, values):
        values = [v.astype(jnp.bfloat16).astype(jnp.float32) for v in values]
        scale = steps / values[2]
        for q in range(2):
            smooth[i, q, part_of(p), :] = (values[q] * scale).astype(jnp.bfloat16)

    def interior(p, i):
        ratios(p, i, [
            0.25 * line(p, q, i - 1) + 0.5 * line(p, q, i) + 0.25 * line(p, q, i + 1) for q in range(3)
        ])

    def border(p, side):
        at, inside = ((0, 1), (rows - 1, rows - 2))[side]
        inner = [0.5 * line(p, q, at) + 0.25 * line(p, q, inside) for q in range(3)]
        for q in range(3):
            partial[side, q, part_of(p), :] = inner[q].astype(jnp.bfloat16)
            edge[1 - side, q, part_of(p), :] = (0.25 * line(p, q, at)).astype(jnp.bfloat16)
        ratios(p, at, inner)

    def joined(side):
        at, inside = ((0, 1), (rows - 1, rows - 2))[side]
        for p in range(PIECES):
            ratios(p, at, [
                0.25 * halo[side, q, part_of(p), :] + 0.5 * line(p, q, at) + 0.25 * line(p, q, inside)
                for q in range(3)
            ])

    def halo_copy(side):
        return pltpu.make_async_remote_copy(
            src_ref=corr.at[:, pl.ds((rows - 1, 0)[side] * chunks, chunks), :],
            dst_ref=halo.at[side],
            send_sem=halo_send,
            recv_sem=halo_recv,
            device_id={"row": (after, before)[side]},
        )

    def row_copy(target, source, sem):
        return pltpu.make_async_remote_copy(
            src_ref=smooth.at[target],
            dst_ref=recv.at[source],
            send_sem=send_sem.at[sem],
            recv_sem=recv_sem.at[source],
            device_id={"angle": target},
        )

    def part_copy(side):
        return pltpu.make_async_remote_copy(
            src_ref=partial.at[side],
            dst_ref=both.at[me, 0],
            send_sem=send_sem.at[1 + side],
            recv_sem=recv_sem.at[me],
            device_id={"angle": (0, last)[side]},
        )

    def edge_copy(side):
        return pltpu.make_async_remote_copy(
            src_ref=edge.at[side],
            dst_ref=both.at[me, 1],
            send_sem=send_sem.at[3 + side],
            recv_sem=recv_sem.at[me],
            device_id=({"angle": 0, "row": after}, {"angle": last, "row": before})[side],
        )

    crossing = (cross_before, cross_after)
    outward = (cross_after, cross_before)

    def border_copies(side):
        target = (0, last)[side]

        @pl.when(crossing[side] & (me != target))
        def _():
            part_copy(side).start()

        @pl.when(jnp.logical_not(crossing[side]) & (me != target))
        def _():
            row_copy(target, me, 1 + side).start()

    def edge_start(side):
        @pl.when(outward[side])
        def _():
            edge_copy(side).start()

    def tell(a):
        pl.semaphore_signal(ready.at[me], inc=1, device_id={"angle": a})

    def upward(t):
        pl.semaphore_wait(ready.at[t], 1)
        row_copy(t, me, 0).start()

    for p in range(PIECES - 1):
        raw_copy(p).wait()
        loop(0, rows // TILE, lambda g: correlate(p, g))
        border(p, 0)
        border(p, 1)
        loop(1, rows - 1, lambda i: interior(p, i))

    p = PIECES - 1
    raw_copy(p).wait()
    loop(0, rows // TILE, lambda g: correlate(p, g))
    border(p, 0)
    border(p, 1)
    pl.semaphore_wait(barrier, me + has_before.astype(jnp.int32) + has_after.astype(jnp.int32))

    @pl.when(even)
    def _():
        halo_copy(0).start()
        border_copies(0)

    @pl.when(odd)
    def _():
        halo_copy(1).start()
        edge_start(0)

    loop(0, me, tell)
    loop(1, rows - 1, lambda i: interior(p, i))
    loop(1, jnp.minimum(me, last), lambda t: row_copy(t, me, 0).start())

    @pl.when(even)
    def _():
        edge_start(1)

    @pl.when(odd)
    def _():
        halo_copy(0).wait_recv()
        joined(0)
        border_copies(0)

    loop(jnp.maximum(me + 1, 1), last, upward)

    @pl.when(even)
    def _():
        halo_copy(1).wait_recv()
        joined(1)

    @pl.when(me < last)
    def _():
        pl.semaphore_wait(ready.at[last], 1)

    border_copies(1)

    flat_copy.wait()
    for q in range(2):
        for c in range(chunks):
            flat_rows[q, c : c + 1, :] = flat_ref[q : q + 1, c * LANES : (c + 1) * LANES].astype(jnp.float32)
    partner_copy.wait()
    table_copy.wait()

    @pl.when(jnp.logical_not(merged))
    def _():
        recv[me] = smooth[me]

    @pl.when(first_row)
    def _():
        both[me, 0] = partial[0]

    @pl.when(last_row)
    def _():
        both[me, 0] = partial[1]

    backward = LANES - 1 - lax.broadcasted_iota(jnp.int32, (TILE, LANES), 1)

    def arrived(a):
        @pl.when(merged)
        def _():
            @pl.when(a != me)
            def _():
                pltpu.make_async_remote_copy(
                    src_ref=both.at[a], dst_ref=both.at[a], send_sem=send_sem.at[0],
                    recv_sem=recv_sem.at[a], device_id={"angle": a},
                ).wait_recv()

            @pl.when(a == me)
            def _():
                pltpu.make_async_remote_copy(
                    src_ref=both.at[a, 1], dst_ref=both.at[a, 1], send_sem=send_sem.at[0],
                    recv_sem=recv_sem.at[a], device_id={"row": after},
                ).wait_recv()

            values = [both[a, 0, q].astype(jnp.float32) + both[a, 1, q].astype(jnp.float32) for q in range(3)]
            scale = steps / values[2]
            for q in range(2):
                recv[a, q] = (values[q] * scale).astype(jnp.bfloat16)

        @pl.when(jnp.logical_not(merged) & (a != me))
        def _():
            row_copy(a, a, 0).wait_recv()

        sine, cosine = recv[a, 1].astype(jnp.float32), recv[a, 0].astype(jnp.float32)
        value = sine * flat_rows[0] - cosine * flat_rows[1]
        dpc = value.astype(jnp.bfloat16).astype(jnp.float32)
        natural[a] = dpc
        for c in range(0, chunks, TILE):
            mirrored[a, c : c + TILE, :] = -jnp.take_along_axis(dpc[c : c + TILE], backward, axis=1)

    stride = jnp.where(me < angles // 2, 1, angles - 1)
    loop(0, angles, lambda k: arrived(lax.rem(me + k * stride, angles)))

    turns = 2 * own
    halves = WIDTH // LANES

    def place(g):
        base = aligned(g * TILE, TILE)
        for c in range(0, chunks, TILE):
            here = jnp.swapaxes(jnp.stack([natural[base + j, c : c + TILE, :] for j in range(TILE)]), 0, 1)
            there = jnp.swapaxes(
                jnp.stack([mirrored[partner_ref[base + j], c : c + TILE, :] for j in range(TILE)]), 0, 1
            )
            for j in range(TILE):
                block, half = divmod(c + j, halves)
                back, turned = own - 1 - block, halves - 1 - half
                lanes = slice(half * LANES, (half + 1) * LANES)
                flipped = slice(turned * LANES, (turned + 1) * LANES)
                ring[pl.ds((own + block) * angles + base, TILE), lanes] = here[j]
                ring[pl.ds(back * angles + base, TILE), flipped] = there[j]
                ring[pl.ds((turns + back) * angles + base, TILE), flipped] = there[j]

    loop(0, angles // TILE, place)

    total = jnp.zeros((own * angles, WIDTH), jnp.float32)
    for m in range(turns):
        first = (own - m) % turns
        window = ring[first * angles : (first + own) * angles].astype(jnp.bfloat16)
        total = total + jnp.dot(window, table[m], preferred_element_type=jnp.float32)
    for block in range(own):
        out_ref[:, block * WIDTH : (block + 1) * WIDTH] = total[
            block * angles : (block + 1) * angles
        ].astype(jnp.bfloat16)

    def rows_sent(count):
        pltpu.make_async_remote_copy(
            src_ref=smooth.at[pl.ds(0, count)], dst_ref=smooth.at[pl.ds(0, count)],
            send_sem=send_sem.at[0], recv_sem=recv_sem.at[0], device_id={"row": after},
        ).wait_send()

    inside = (me > 0) & (me < last)

    @pl.when(inside)
    def _():
        rows_sent(angles - 3)

    @pl.when(jnp.logical_not(inside))
    def _():
        rows_sent(angles - 2)

    for side in range(2):
        target = (0, last)[side]

        @pl.when(crossing[side] & (me != target))
        def _():
            part_copy(side).wait_send()

        @pl.when(jnp.logical_not(crossing[side]) & (me != target))
        def _():
            row_copy(target, me, 1 + side).wait_send()

        @pl.when(outward[side])
        def _():
            edge_copy(side).wait_send()

    halo_copy(0).wait_send()


def local(raw_frames, step_index, partner, flat_field):
    _, steps, rows, det = raw_frames.shape
    angles = lax.axis_size("angle")
    blocks_row = lax.axis_size("row")
    chunks = det // LANES
    own = det // WIDTH
    assert rows == angles and rows % TILE == 0 and blocks_row % 2 == 0 and raw_frames.shape[0] == 1
    table = jnp.asarray(circulant_blocks(2 * det))
    body = lambda *refs: kernel(angles, blocks_row, *refs)
    result = pl.pallas_call(
        body,
        out_shape=jax.ShapeDtypeStruct((angles, det), jnp.bfloat16),
        in_specs=[pl.BlockSpec(memory_space=pltpu.HBM)] * 5,
        out_specs=pl.BlockSpec(memory_space=pltpu.VMEM),
        scratch_shapes=[
            pltpu.VMEM((steps, rows, det // PIECES), jnp.bfloat16),
            pltpu.VMEM((steps, rows, det // PIECES), jnp.bfloat16),
            pltpu.VMEM(table.shape, jnp.bfloat16),
            pltpu.SMEM((1, steps), jnp.int32),
            pltpu.SMEM((angles,), jnp.int32),
            pltpu.VMEM((2, det), jnp.bfloat16),
            pltpu.VMEM((2, chunks, LANES), jnp.float32),
            pltpu.VMEM((3, rows * chunks, LANES), jnp.float32),
            pltpu.VMEM((2, 3, chunks, LANES), jnp.float32),
            pltpu.VMEM((2, 3, chunks, LANES), jnp.bfloat16),
            pltpu.VMEM((2, 3, chunks, LANES), jnp.bfloat16),
            pltpu.VMEM((angles, 2, 3, chunks, LANES), jnp.bfloat16),
            pltpu.VMEM((rows, 2, chunks, LANES), jnp.bfloat16),
            pltpu.VMEM((angles, 2, chunks, LANES), jnp.bfloat16),
            pltpu.VMEM((angles, chunks, LANES), jnp.float32),
            pltpu.VMEM((angles, chunks, LANES), jnp.float32),
            pltpu.VMEM((3 * own * angles, WIDTH), jnp.float32),
            pltpu.SemaphoreType.DMA((4 + PIECES,)),
            pltpu.SemaphoreType.DMA,
            pltpu.SemaphoreType.DMA,
            pltpu.SemaphoreType.DMA((5,)),
            pltpu.SemaphoreType.DMA((angles,)),
            pltpu.SemaphoreType.REGULAR((angles,)),
        ],
        compiler_params=pltpu.CompilerParams(
            collective_id=0, has_side_effects=True, vmem_limit_bytes=48 * 1024 * 1024
        ),
    )(*[pltpu.with_memory_space_constraint(x, pltpu.HBM) for x in (raw_frames, step_index, partner, flat_field[:, 0, :], table)])
    return result[:, None, :]


def solution(mesh):
    in_specs = (
        P("angle", None, "row", None),
        P("angle", None),
        P(),
        P(None, ("row", "angle"), None),
    )
    out_specs = P(None, ("row", "angle"), None)
    return jax.shard_map(local, mesh=mesh, in_specs=in_specs, out_specs=out_specs, check_vma=False)
```

```python
import math

import jax
import jax.numpy as jnp
import ml_dtypes
import numpy as np
from jax import lax
from jax.experimental import pallas as pl
from jax.experimental.pallas import tpu as pltpu
from jax.sharding import PartitionSpec as P

WIDTH = 256
LANES = 128
TILE = 8
PIECES = 2
SPLIT = 4


def circulant_blocks(padlen):
    count = padlen // WIDTH
    n = np.arange(padlen, dtype=np.float64)
    odd = np.arange(padlen) % 2 == 1
    taps = np.where(odd, (2.0 / padlen) / np.tan(np.pi * np.where(odd, n, 1.0) / padlen), 0.0)
    m = np.arange(count)[:, None, None]
    p = np.arange(WIDTH)[None, :, None]
    q = np.arange(WIDTH)[None, None, :]
    return taps[(WIDTH * m + q - p) % padlen].astype(ml_dtypes.bfloat16)


def loop(start, stop, body):
    if isinstance(start, int) and isinstance(stop, int) and stop - start <= 8:
        for i in range(start, stop):
            body(i)
    else:
        lax.fori_loop(start, stop, lambda i, _: body(i), None)


def aligned(value, step):
    return value if isinstance(value, int) else pl.multiple_of(value, step)


def kernel(
    angles, blocks_row, raw_hbm, step_hbm, partner_hbm, flat_hbm, table_hbm, out_ref,
    raw_first, raw_second, table, step_ref, partner_ref, flat_ref, flat_rows, corr, halo, partial, edge, both, smooth, recv, natural, mirrored, ring,
    local_sem, halo_sem, send_sem, recv_sem, ready,
):
    raw = (raw_first, raw_second)
    steps, rows, _ = raw_first.shape
    det = flat_ref.shape[1]
    chunks = det // LANES
    per = chunks // PIECES
    own = det // WIDTH
    last = angles - 1
    me = lax.axis_index("angle")
    row = lax.axis_index("row")
    after = lax.rem(row + 1, blocks_row)
    before = lax.rem(row + blocks_row - 1, blocks_row)
    has_before = row > 0
    has_after = row < blocks_row - 1
    odd = lax.rem(row, 2) == 1
    even = jnp.logical_not(odd)
    cross_before = has_before & even
    cross_after = has_after & odd
    first_row = (me == 0) & cross_before
    last_row = (me == last) & cross_after
    merged = first_row | last_row

    barrier = pltpu.get_barrier_semaphore()

    step_copy = pltpu.make_async_copy(step_hbm, step_ref, local_sem.at[0])
    step_copy.start()

    def raw_copy(p, part, parts):
        width = per * LANES // parts
        return pltpu.make_async_copy(
            raw_hbm.at[0, :, :, pl.ds(p * per * LANES + part * width, width)],
            raw[p].at[:, :, pl.ds(part * width, width)],
            local_sem.at[1 + p],
        )

    for p in range(PIECES):
        for part in range(SPLIT):
            raw_copy(p, part, SPLIT).start()

    def greet(a):
        pl.semaphore_signal(barrier, inc=1, device_id={"angle": a})

    loop(me + 1, angles, greet)

    @pl.when(even)
    def _():
        pl.semaphore_signal(barrier, inc=1, device_id={"row": after})

    @pl.when(odd)
    def _():
        pl.semaphore_signal(barrier, inc=1, device_id={"row": before})

    @pl.when(first_row)
    def _():
        loop(0, angles, lambda a: pl.semaphore_signal(
            barrier, inc=1, device_id={"angle": a, "row": before}
        ))

    @pl.when(last_row)
    def _():
        loop(0, angles, lambda a: pl.semaphore_signal(
            barrier, inc=1, device_id={"angle": a, "row": after}
        ))

    step_copy.wait()
    flat_copy = pltpu.make_async_copy(flat_hbm, flat_ref, local_sem.at[0])
    flat_copy.start()
    partner_copy = pltpu.make_async_copy(partner_hbm, partner_ref, local_sem.at[1])
    table_copy = pltpu.make_async_copy(table_hbm, table, local_sem.at[2])

    named = [step_ref[0, k] for k in range(steps)]
    frame_of = []
    for i in range(steps):
        at = jnp.int32(0)
        for k in range(1, steps):
            at = jnp.where(named[k] == i, jnp.int32(k), at)
        frame_of.append(at)
    assert steps == 8
    half_root = float(np.float32(math.sqrt(0.5)))

    def correlate(p, g):
        at = aligned(g * TILE, TILE)
        sums = [[], [], []]
        for c in range(per):
            f = [
                raw[p][frame_of[i], pl.ds(at, TILE), c * LANES : (c + 1) * LANES].astype(jnp.float32)
                for i in range(steps)
            ]
            less = [f[i] - f[i + 4] for i in range(4)]
            more = [f[i] + f[i + 4] for i in range(4)]
            sums[0].append(less[0] + (less[1] - less[3]) * half_root)
            sums[1].append(less[2] + (less[1] + less[3]) * half_root)
            sums[2].append((more[0] + more[2]) + (more[1] + more[3]))
        for q in range(3):
            turned = jnp.swapaxes(jnp.stack(sums[q]), 0, 1)
            for j in range(TILE):
                corr[q, pl.ds(aligned((at + j) * chunks + p * per, TILE), per), :] = turned[j]

    def line(p, q, i):
        return corr[q, pl.ds(aligned(i * chunks + p * per, TILE), per), :]

    def part_of(p):
        return slice(p * per, (p + 1) * per)

    def ratios(p, i, values):
        values = [v.astype(jnp.bfloat16).astype(jnp.float32) for v in values]
        scale = steps / values[2]
        for q in range(2):
            smooth[i, q, part_of(p), :] = (values[q] * scale).astype(jnp.bfloat16)

    def interior(p, i):
        ratios(p, i, [
            0.25 * line(p, q, i - 1) + 0.5 * line(p, q, i) + 0.25 * line(p, q, i + 1) for q in range(3)
        ])

    def border(p, side):
        at, inside = ((0, 1), (rows - 1, rows - 2))[side]
        inner = [0.5 * line(p, q, at) + 0.25 * line(p, q, inside) for q in range(3)]
        for q in range(3):
            partial[side, q, part_of(p), :] = inner[q].astype(jnp.bfloat16)
        ratios(p, at, inner)

    def rim(p, side):
        for q in range(3):
            edge[side, q, part_of(p), :] = (0.25 * line(p, q, (rows - 1, 0)[side])).astype(jnp.bfloat16)

    def joined(side):
        at, inside = ((0, 1), (rows - 1, rows - 2))[side]
        for p in range(PIECES):
            ratios(p, at, [
                halo[q, part_of(p), :].astype(jnp.float32) + 0.5 * line(p, q, at) + 0.25 * line(p, q, inside)
                for q in range(3)
            ])

    def halo_copy(side):
        return pltpu.make_async_remote_copy(
            src_ref=edge.at[side],
            dst_ref=halo,
            send_sem=send_sem,
            recv_sem=halo_sem,
            device_id={"row": (after, before)[side]},
        )

    def row_copy(target, source):
        return pltpu.make_async_remote_copy(
            src_ref=smooth.at[target],
            dst_ref=recv.at[source],
            send_sem=send_sem,
            recv_sem=recv_sem.at[source],
            device_id={"angle": target},
        )

    def part_copy(side):
        return pltpu.make_async_remote_copy(
            src_ref=partial.at[side],
            dst_ref=both.at[pl.ds(me * 6, 3)],
            send_sem=send_sem,
            recv_sem=recv_sem.at[me],
            device_id={"angle": (0, last)[side]},
        )

    def edge_copy(side):
        return pltpu.make_async_remote_copy(
            src_ref=edge.at[side],
            dst_ref=both.at[pl.ds(me * 6 + 3, 3)],
            send_sem=send_sem,
            recv_sem=recv_sem.at[me],
            device_id=({"angle": 0, "row": after}, {"angle": last, "row": before})[side],
        )

    crossing = (cross_before, cross_after)
    outward = (cross_after, cross_before)

    def border_copies(side):
        target = (0, last)[side]

        @pl.when(crossing[side] & (me != target))
        def _():
            part_copy(side).start()

        @pl.when(jnp.logical_not(crossing[side]) & (me != target))
        def _():
            row_copy(target, me).start()

    def edge_start(side):
        @pl.when(outward[side])
        def _():
            edge_copy(side).start()

    def tell(a):
        pl.semaphore_signal(ready.at[(me == last).astype(jnp.int32)], inc=1, device_id={"angle": a})


    for p in range(PIECES):
        raw_copy(p, 0, 1).wait()
        (partner_copy, table_copy)[p].start()
        loop(0, rows // TILE, lambda g: correlate(p, g))

    for p in range(PIECES):
        border(p, 0)
        rim(p, 0)

    pl.semaphore_wait(barrier, me + has_before.astype(jnp.int32) + has_after.astype(jnp.int32))

    @pl.when(even)
    def _():
        border_copies(0)
        halo_copy(0).start()

    @pl.when(odd)
    def _():
        edge_start(0)

    loop(0, me, tell)
    for p in range(PIECES):
        loop(1, rows - 1, lambda i: interior(p, i))
        border(p, 1)
        rim(p, 1)

    @pl.when(odd)
    def _():
        halo_copy(1).start()

    def bulk():
        loop(1, jnp.minimum(me, last), lambda t: row_copy(t, me).start())

    @pl.when(even)
    def _():
        bulk()
        edge_start(1)

    @pl.when(odd)
    def _():
        halo_copy(0).wait_recv()
        joined(0)
        border_copies(0)
        bulk()

    @pl.when(me < last - 1)
    def _():
        pl.semaphore_wait(ready.at[0], last - 1 - me)

    loop(me + 1, last, lambda t: row_copy(t, me).start())


    @pl.when(even)
    def _():
        halo_copy(1).wait_recv()
        joined(1)

    @pl.when(me < last)
    def _():
        pl.semaphore_wait(ready.at[1], 1)

    border_copies(1)

    flat_copy.wait()
    for q in range(2):
        for c in range(chunks):
            flat_rows[q, c : c + 1, :] = flat_ref[q : q + 1, c * LANES : (c + 1) * LANES].astype(jnp.float32)
    partner_copy.wait()
    table_copy.wait()

    @pl.when(jnp.logical_not(merged))
    def _():
        recv[me] = smooth[me]

    @pl.when(first_row)
    def _():
        both[pl.ds(me * 6, 3)] = partial[0]

    @pl.when(last_row)
    def _():
        both[pl.ds(me * 6, 3)] = partial[1]

    backward = LANES - 1 - lax.broadcasted_iota(jnp.int32, (TILE, LANES), 1)

    def arrived(a):
        @pl.when(merged)
        def _():
            @pl.when(a != me)
            def _():
                pltpu.make_async_remote_copy(
                    src_ref=both.at[pl.ds(a * 6, 6)], dst_ref=both.at[pl.ds(a * 6, 6)], send_sem=send_sem,
                    recv_sem=recv_sem.at[a], device_id={"angle": a},
                ).wait_recv()

            @pl.when(a == me)
            def _():
                pltpu.make_async_remote_copy(
                    src_ref=edge.at[0], dst_ref=both.at[pl.ds(a * 6 + 3, 3)], send_sem=send_sem,
                    recv_sem=recv_sem.at[a], device_id={"row": after},
                ).wait_recv()

            values = [both[a * 6 + q].astype(jnp.float32) + both[a * 6 + 3 + q].astype(jnp.float32) for q in range(3)]
            scale = steps / values[2]
            for q in range(2):
                recv[a, q] = (values[q] * scale).astype(jnp.bfloat16)

        @pl.when(jnp.logical_not(merged) & (a != me))
        def _():
            row_copy(a, a).wait_recv()

        sine, cosine = recv[a, 1].astype(jnp.float32), recv[a, 0].astype(jnp.float32)
        value = sine * flat_rows[0] - cosine * flat_rows[1]
        dpc = value.astype(jnp.bfloat16).astype(jnp.float32)
        natural[a] = dpc
        for c in range(0, chunks, TILE):
            mirrored[a, c : c + TILE, :] = -jnp.take_along_axis(dpc[c : c + TILE], backward, axis=1)

    stride = jnp.where(me < angles // 2, 1, angles - 1)
    loop(0, angles, lambda k: arrived(lax.rem(me + k * stride, angles)))

    turns = 2 * own
    halves = WIDTH // LANES

    def place(g):
        base = aligned(g * TILE, TILE)
        for c in range(0, chunks, TILE):
            here = jnp.swapaxes(jnp.stack([natural[base + j, c : c + TILE, :] for j in range(TILE)]), 0, 1)
            there = jnp.swapaxes(
                jnp.stack([mirrored[partner_ref[base + j], c : c + TILE, :] for j in range(TILE)]), 0, 1
            )
            for j in range(TILE):
                block, half = divmod(c + j, halves)
                back, turned = own - 1 - block, halves - 1 - half
                lanes = slice(half * LANES, (half + 1) * LANES)
                flipped = slice(turned * LANES, (turned + 1) * LANES)
                ring[pl.ds((own + block) * angles + base, TILE), lanes] = here[j]
                ring[pl.ds(back * angles + base, TILE), flipped] = there[j]
                ring[pl.ds((turns + back) * angles + base, TILE), flipped] = there[j]

    loop(0, angles // TILE, place)

    total = jnp.zeros((own * angles, WIDTH), jnp.float32)
    for m in range(turns):
        first = (own - m) % turns
        window = ring[first * angles : (first + own) * angles].astype(jnp.bfloat16)
        total = total + jnp.dot(window, table[m], preferred_element_type=jnp.float32)
    for block in range(own):
        out_ref[:, block * WIDTH : (block + 1) * WIDTH] = total[
            block * angles : (block + 1) * angles
        ].astype(jnp.bfloat16)

    crossed = cross_before | cross_after

    def sent(units):
        pltpu.make_async_remote_copy(
            src_ref=both.at[pl.ds(0, units)], dst_ref=both.at[pl.ds(0, units)],
            send_sem=send_sem, recv_sem=halo_sem, device_id={"row": after},
        ).wait_send()

    @pl.when(jnp.logical_not(crossed))
    def _():
        sent(2 * angles + 1)

    @pl.when(crossed & jnp.logical_not(merged))
    def _():
        sent(2 * angles + 5)

    @pl.when(merged)
    def _():
        sent(2 * angles + 4)


def local(raw_frames, step_index, partner, flat_field):
    _, steps, rows, det = raw_frames.shape
    angles = lax.axis_size("angle")
    blocks_row = lax.axis_size("row")
    chunks = det // LANES
    own = det // WIDTH
    assert rows == angles and rows % TILE == 0 and blocks_row % 2 == 0 and raw_frames.shape[0] == 1
    table = jnp.asarray(circulant_blocks(2 * det))
    body = lambda *refs: kernel(angles, blocks_row, *refs)
    result = pl.pallas_call(
        body,
        out_shape=jax.ShapeDtypeStruct((angles, det), jnp.bfloat16),
        in_specs=[pl.BlockSpec(memory_space=pltpu.HBM)] * 5,
        out_specs=pl.BlockSpec(memory_space=pltpu.VMEM),
        scratch_shapes=[
            pltpu.VMEM((steps, rows, det // PIECES), jnp.bfloat16),
            pltpu.VMEM((steps, rows, det // PIECES), jnp.bfloat16),
            pltpu.VMEM(table.shape, jnp.bfloat16),
            pltpu.SMEM((1, steps), jnp.int32),
            pltpu.SMEM((angles,), jnp.int32),
            pltpu.VMEM((2, det), jnp.bfloat16),
            pltpu.VMEM((2, chunks, LANES), jnp.float32),
            pltpu.VMEM((3, rows * chunks, LANES), jnp.float32),
            pltpu.VMEM((3, chunks, LANES), jnp.bfloat16),
            pltpu.VMEM((2, 3, chunks, LANES), jnp.bfloat16),
            pltpu.VMEM((2, 3, chunks, LANES), jnp.bfloat16),
            pltpu.VMEM((angles * 6, chunks, LANES), jnp.bfloat16),
            pltpu.VMEM((rows, 2, chunks, LANES), jnp.bfloat16),
            pltpu.VMEM((angles, 2, chunks, LANES), jnp.bfloat16),
            pltpu.VMEM((angles, chunks, LANES), jnp.float32),
            pltpu.VMEM((angles, chunks, LANES), jnp.float32),
            pltpu.VMEM((3 * own * angles, WIDTH), jnp.float32),
            pltpu.SemaphoreType.DMA((1 + PIECES,)),
            pltpu.SemaphoreType.DMA,
            pltpu.SemaphoreType.DMA,
            pltpu.SemaphoreType.DMA((angles,)),
            pltpu.SemaphoreType.REGULAR((2,)),
        ],
        compiler_params=pltpu.CompilerParams(
            collective_id=0, has_side_effects=True, vmem_limit_bytes=48 * 1024 * 1024
        ),
    )(*[pltpu.with_memory_space_constraint(x, pltpu.HBM) for x in (raw_frames, step_index, partner, flat_field[:, 0, :], table)])
    return result[:, None, :]


def solution(mesh):
    in_specs = (
        P("angle", None, "row", None),
        P("angle", None),
        P(),
        P(None, ("row", "angle"), None),
    )
    out_specs = P(None, ("row", "angle"), None)
    return jax.shard_map(local, mesh=mesh, in_specs=in_specs, out_specs=out_specs, check_vma=False)
```

```python
import math

import jax
import jax.numpy as jnp
import ml_dtypes
import numpy as np
from jax import lax
from jax.experimental import pallas as pl
from jax.experimental.pallas import tpu as pltpu
from jax.sharding import PartitionSpec as P

WIDTH = 256
LANES = 128
TILE = 8
PIECES = 2
SPLIT = 4
GROUPS = 4


def circulant_blocks(padlen):
    count = padlen // (2 * WIDTH)
    n = np.arange(padlen, dtype=np.float64)
    odd = np.arange(padlen) % 2 == 1
    taps = np.where(odd, (2.0 / padlen) / np.tan(np.pi * np.where(odd, n, 1.0) / padlen), 0.0)
    m = np.arange(count)[:, None, None]
    p = np.arange(WIDTH)[None, :, None]
    q = np.arange(WIDTH)[None, None, :]
    return taps[(2 * (WIDTH * m + q - p) - 1) % padlen].astype(ml_dtypes.bfloat16)


def loop(start, stop, body):
    if isinstance(start, int) and isinstance(stop, int) and stop - start <= 8:
        for i in range(start, stop):
            body(i)
    else:
        lax.fori_loop(start, stop, lambda i, _: body(i), None)


def aligned(value, step):
    return value if isinstance(value, int) else pl.multiple_of(value, step)


def kernel(
    angles, blocks_row, raw_hbm, step_hbm, partner_hbm, flat_hbm, table_hbm, out_ref,
    raw_first, raw_second, table, step_ref, partner_ref, flat_ref, flat_rows, corr, halo, partial, edge, both, smooth, recv, natural, mirrored, tiles, ring,
    local_sem, halo_sem, send_sem, recv_sem, ready,
):
    raw = (raw_first, raw_second)
    steps, rows, _ = raw_first.shape
    det = flat_ref.shape[1]
    chunks = det // LANES
    per = chunks // PIECES
    own = det // (2 * WIDTH)
    last = angles - 1
    me = lax.axis_index("angle")
    row = lax.axis_index("row")
    after = lax.rem(row + 1, blocks_row)
    before = lax.rem(row + blocks_row - 1, blocks_row)
    has_before = row > 0
    has_after = row < blocks_row - 1
    odd = lax.rem(row, 2) == 1
    even = jnp.logical_not(odd)
    cross_before = has_before & even
    cross_after = has_after & odd
    first_row = (me == 0) & cross_before
    last_row = (me == last) & cross_after
    merged = first_row | last_row

    final = jnp.where(me < angles // 2, last, 0)

    def landing(target):
        other = jnp.where(target < angles // 2, last, 0)
        return recv_sem.at[(me == other).astype(jnp.int32)]

    barrier = pltpu.get_barrier_semaphore()

    step_copy = pltpu.make_async_copy(step_hbm, step_ref, local_sem.at[0])
    step_copy.start()

    def raw_copy(p, part, parts):
        width = per * LANES // parts
        return pltpu.make_async_copy(
            raw_hbm.at[0, :, :, pl.ds(p * per * LANES + part * width, width)],
            raw[p].at[:, :, pl.ds(part * width, width)],
            local_sem.at[1 + p],
        )

    for p in range(PIECES):
        for part in range(SPLIT):
            raw_copy(p, part, SPLIT).start()

    def greet(a):
        pl.semaphore_signal(barrier, inc=1, device_id={"angle": a})

    loop(me + 1, angles, greet)

    @pl.when(even)
    def _():
        pl.semaphore_signal(barrier, inc=1, device_id={"row": after})

    @pl.when(odd)
    def _():
        pl.semaphore_signal(barrier, inc=1, device_id={"row": before})

    @pl.when(first_row)
    def _():
        loop(0, angles, lambda a: pl.semaphore_signal(
            barrier, inc=1, device_id={"angle": a, "row": before}
        ))

    @pl.when(last_row)
    def _():
        loop(0, angles, lambda a: pl.semaphore_signal(
            barrier, inc=1, device_id={"angle": a, "row": after}
        ))

    step_copy.wait()
    flat_copy = pltpu.make_async_copy(flat_hbm, flat_ref, local_sem.at[0])
    flat_copy.start()
    partner_copy = pltpu.make_async_copy(partner_hbm, partner_ref, local_sem.at[1])
    table_copy = pltpu.make_async_copy(table_hbm, table, local_sem.at[2])

    named = [step_ref[0, k] for k in range(steps)]
    frame_of = []
    for i in range(steps):
        at = jnp.int32(0)
        for k in range(1, steps):
            at = jnp.where(named[k] == i, jnp.int32(k), at)
        frame_of.append(at)
    assert steps == 8
    half_root = float(np.float32(math.sqrt(0.5)))

    def correlate(p, g):
        at = aligned(g * TILE, TILE)
        sums = [[], [], []]
        for c in range(per):
            f = [
                raw[p][frame_of[i], pl.ds(at, TILE), c * LANES : (c + 1) * LANES].astype(jnp.float32)
                for i in range(steps)
            ]
            less = [f[i] - f[i + 4] for i in range(4)]
            more = [f[i] + f[i + 4] for i in range(4)]
            sums[0].append(less[0] + (less[1] - less[3]) * half_root)
            sums[1].append(less[2] + (less[1] + less[3]) * half_root)
            sums[2].append((more[0] + more[2]) + (more[1] + more[3]))
        for q in range(3):
            turned = jnp.swapaxes(jnp.stack(sums[q]), 0, 1)
            for j in range(TILE):
                corr[q, pl.ds(aligned((at + j) * chunks + p * per, TILE), per), :] = turned[j]

    def line(p, q, i):
        return corr[q, pl.ds(aligned(i * chunks + p * per, TILE), per), :]

    def part_of(p):
        return slice(p * per, (p + 1) * per)

    def ratios(p, i, values):
        values = [v.astype(jnp.bfloat16).astype(jnp.float32) for v in values]
        scale = steps / values[2]
        for q in range(2):
            smooth[i, q, part_of(p), :] = (values[q] * scale).astype(jnp.bfloat16)

    def interior(p, i):
        ratios(p, i, [
            0.25 * line(p, q, i - 1) + 0.5 * line(p, q, i) + 0.25 * line(p, q, i + 1) for q in range(3)
        ])

    def border(p, side):
        at, inside = ((0, 1), (rows - 1, rows - 2))[side]
        inner = [0.5 * line(p, q, at) + 0.25 * line(p, q, inside) for q in range(3)]
        for q in range(3):
            partial[side, q, part_of(p), :] = inner[q].astype(jnp.bfloat16)
        ratios(p, at, inner)

    def rim(p, side):
        for q in range(3):
            edge[side, q, part_of(p), :] = (0.25 * line(p, q, (rows - 1, 0)[side])).astype(jnp.bfloat16)

    def joined(side):
        at, inside = ((0, 1), (rows - 1, rows - 2))[side]
        for p in range(PIECES):
            ratios(p, at, [
                halo[q, part_of(p), :].astype(jnp.float32) + 0.5 * line(p, q, at) + 0.25 * line(p, q, inside)
                for q in range(3)
            ])

    def halo_copy(side):
        return pltpu.make_async_remote_copy(
            src_ref=edge.at[side],
            dst_ref=halo,
            send_sem=send_sem,
            recv_sem=halo_sem,
            device_id={"row": (after, before)[side]},
        )

    def row_copy(target):
        return pltpu.make_async_remote_copy(
            src_ref=smooth.at[target],
            dst_ref=recv.at[me],
            send_sem=send_sem,
            recv_sem=landing(target),
            device_id={"angle": target},
        )

    def part_copy(side):
        return pltpu.make_async_remote_copy(
            src_ref=partial.at[side],
            dst_ref=both.at[pl.ds(me * 6, 3)],
            send_sem=send_sem,
            recv_sem=landing((0, last)[side]),
            device_id={"angle": (0, last)[side]},
        )

    def edge_copy(side):
        return pltpu.make_async_remote_copy(
            src_ref=edge.at[side],
            dst_ref=both.at[pl.ds(me * 6 + 3, 3)],
            send_sem=send_sem,
            recv_sem=landing((0, last)[side]),
            device_id=({"angle": 0, "row": after}, {"angle": last, "row": before})[side],
        )

    crossing = (cross_before, cross_after)
    outward = (cross_after, cross_before)

    def border_copies(side):
        target = (0, last)[side]

        @pl.when(crossing[side] & (me != target))
        def _():
            part_copy(side).start()

        @pl.when(jnp.logical_not(crossing[side]) & (me != target))
        def _():
            row_copy(target).start()

    def edge_start(side):
        @pl.when(outward[side])
        def _():
            edge_copy(side).start()

    reach = angles // GROUPS

    def tell(a):
        pl.semaphore_signal(ready.at[me // reach], inc=1, device_id={"angle": a})


    for p in range(PIECES):
        raw_copy(p, 0, 1).wait()
        (partner_copy, table_copy)[p].start()
        loop(0, rows // TILE, lambda g: correlate(p, g))

    for p in range(PIECES):
        border(p, 0)
        rim(p, 0)

    pl.semaphore_wait(barrier, me + has_before.astype(jnp.int32) + has_after.astype(jnp.int32))

    @pl.when(even)
    def _():
        border_copies(0)
        halo_copy(0).start()

    @pl.when(odd)
    def _():
        edge_start(0)

    loop(0, me, tell)
    for p in range(PIECES):
        loop(1, rows - 1, lambda i: interior(p, i))
        border(p, 1)
        rim(p, 1)

    @pl.when(odd)
    def _():
        halo_copy(1).start()

    def bulk():
        loop(1, jnp.minimum(me, last), lambda t: row_copy(t).start())

    @pl.when(even)
    def _():
        bulk()
        edge_start(1)

    @pl.when(odd)
    def _():
        halo_copy(0).wait_recv()
        joined(0)
        border_copies(0)
        bulk()

    @pl.when(even)
    def _():
        halo_copy(1).wait_recv()
        joined(1)

    for group in range(GROUPS):
        low, high = jnp.maximum(me + 1, group * reach), (group + 1) * reach

        @pl.when(low < high)
        def _():
            pl.semaphore_wait(ready.at[group], high - low)
            loop(low, min(high, last), lambda t: row_copy(t).start())

    border_copies(1)

    flat_copy.wait()
    for q in range(2):
        for c in range(chunks):
            flat_rows[q, c : c + 1, :] = flat_ref[q : q + 1, c * LANES : (c + 1) * LANES].astype(jnp.float32)
    partner_copy.wait()
    table_copy.wait()

    @pl.when(jnp.logical_not(merged))
    def _():
        recv[me] = smooth[me]

    @pl.when(first_row)
    def _():
        both[pl.ds(me * 6, 3)] = partial[0]

    @pl.when(last_row)
    def _():
        both[pl.ds(me * 6, 3)] = partial[1]

    lane = lax.broadcasted_iota(jnp.int32, (TILE, LANES), 1)
    sublane = lax.broadcasted_iota(jnp.int32, (TILE, LANES), 0)
    middle = LANES // 2
    lower = lane < middle
    paired = 2 * jnp.where(lower, lane, lane - middle)
    odd_first = lower == (lax.rem(sublane, 2) == 0)
    onward = paired + odd_first.astype(jnp.int32)
    backward = LANES - 2 - paired + odd_first.astype(jnp.int32)

    def landed(at, units):
        pltpu.make_async_remote_copy(
            src_ref=both.at[pl.ds(0, units)], dst_ref=both.at[pl.ds(0, units)],
            send_sem=send_sem, recv_sem=recv_sem.at[at], device_id={"row": after},
        ).wait_recv()

    def merge(a):
        values = [both[a * 6 + q].astype(jnp.float32) + both[a * 6 + 3 + q].astype(jnp.float32) for q in range(3)]
        scale = steps / values[2]
        for q in range(2):
            recv[a, q] = (values[q] * scale).astype(jnp.bfloat16)

    def differ(a):
        sine, cosine = recv[a, 1].astype(jnp.float32), recv[a, 0].astype(jnp.float32)
        value = sine * flat_rows[0] - cosine * flat_rows[1]
        dpc = value.astype(jnp.bfloat16).astype(jnp.float32)
        for c in range(0, chunks, TILE):
            natural[a, c : c + TILE, :] = jnp.take_along_axis(dpc[c : c + TILE], onward, axis=1)
            mirrored[a, c : c + TILE, :] = -jnp.take_along_axis(dpc[c : c + TILE], backward, axis=1)

    def others(body):
        loop(0, last, lambda k: body(lax.rem(final + 1 + k, angles)))

    @pl.when(merged)
    def _():
        landed(0, 6 * (angles - 2) + 3)
        others(merge)

    @pl.when(jnp.logical_not(merged))
    def _():
        landed(0, 2 * (angles - 2))

    others(differ)
    natural[final] = jnp.zeros(natural.shape[1:], natural.dtype)
    mirrored[final] = jnp.zeros(mirrored.shape[1:], mirrored.dtype)

    def turn(g):
        base = aligned(g * TILE, TILE)
        for c in range(0, chunks, TILE):
            here = jnp.swapaxes(jnp.stack([natural[base + j, c : c + TILE, :] for j in range(TILE)]), 0, 1)
            there = jnp.swapaxes(
                jnp.stack([mirrored[partner_ref[base + j], c : c + TILE, :] for j in range(TILE)]), 0, 1
            )
            for j in range(TILE):
                tiles[chunks + c + j, pl.ds(base, TILE), :] = here[j]
                tiles[chunks - 1 - c - j, pl.ds(base, TILE), :] = there[j]

    loop(0, angles // TILE, turn)

    @pl.when(merged)
    def _():
        landed(1, 6)
        merge(final)

    @pl.when(jnp.logical_not(merged))
    def _():
        landed(1, 2)

    differ(final)

    def place(g):
        base = aligned(g * TILE, TILE)
        here, there = sublane + base == final, sublane + base == partner_ref[final]

        def tile(c):
            if c < chunks:
                row = mirrored[final, chunks - 1 - c : chunks - c, :]
                return jnp.where(there, row, tiles[c, pl.ds(base, TILE), :])
            row = natural[final, c - chunks : c - chunks + 1, :]
            return jnp.where(here, row, tiles[c, pl.ds(base, TILE), :])

        uneven, turned = [], []
        for block in range(chunks):
            first, second = tile(2 * block), tile(2 * block + 1)
            uneven.append(jnp.where(lower, first, second))
            turned.append(pltpu.roll(jnp.where(lower, second, first), middle - 1, 1))
        for block in range(chunks):
            shifted = jnp.where(lane < LANES - 1, turned[block], turned[(block + 1) % chunks])
            group, half = divmod(block, 2)
            lanes = slice(half * LANES, (half + 1) * LANES)
            for k in (group, group + 2 * own)[: 2 if group < own else 1]:
                ring[pl.ds(2 * k * angles + base, TILE), lanes] = uneven[block]
                ring[pl.ds((2 * k + 1) * angles + base, TILE), lanes] = shifted

    loop(0, angles // TILE, place)

    turns = 2 * own
    height = 2 * own * angles
    total = jnp.zeros((height, WIDTH), jnp.float32)
    for m in range(turns):
        first = ((own - m) % turns) * 2 * angles
        window = ring[first : first + height].astype(jnp.bfloat16)
        total = total + jnp.dot(window, table[m], preferred_element_type=jnp.float32)
    total = total.astype(jnp.bfloat16).astype(jnp.float32)
    second_half = lane // 2 + middle
    for k in range(own):
        for half in range(2):
            lanes = slice(half * LANES, (half + 1) * LANES)
            for base in range(0, angles, TILE):
                at = 2 * k * angles + base
                even_at = total[at : at + TILE, lanes]
                odd_at = total[at + angles : at + angles + TILE, lanes]
                for part, index in enumerate((lane // 2, second_half)):
                    c = 4 * k + 2 * half + part
                    mixed = jnp.where(
                        lax.rem(lane, 2) == 0,
                        jnp.take_along_axis(even_at, index, axis=1),
                        jnp.take_along_axis(odd_at, index, axis=1),
                    )
                    out_ref[base : base + TILE, c * LANES : (c + 1) * LANES] = mixed.astype(jnp.bfloat16)

    crossed = cross_before | cross_after

    def sent(units):
        pltpu.make_async_remote_copy(
            src_ref=both.at[pl.ds(0, units)], dst_ref=both.at[pl.ds(0, units)],
            send_sem=send_sem, recv_sem=halo_sem, device_id={"row": after},
        ).wait_send()

    @pl.when(jnp.logical_not(crossed))
    def _():
        sent(2 * angles + 1)

    @pl.when(crossed & jnp.logical_not(merged))
    def _():
        sent(2 * angles + 5)

    @pl.when(merged)
    def _():
        sent(2 * angles + 4)


def local(raw_frames, step_index, partner, flat_field):
    _, steps, rows, det = raw_frames.shape
    angles = lax.axis_size("angle")
    blocks_row = lax.axis_size("row")
    chunks = det // LANES
    own = det // (2 * WIDTH)
    assert rows == angles and rows % TILE == 0 and blocks_row % 2 == 0 and angles % GROUPS == 0 and raw_frames.shape[0] == 1
    table = jnp.asarray(circulant_blocks(2 * det))
    body = lambda *refs: kernel(angles, blocks_row, *refs)
    result = pl.pallas_call(
        body,
        out_shape=jax.ShapeDtypeStruct((angles, det), jnp.bfloat16),
        in_specs=[pl.BlockSpec(memory_space=pltpu.HBM)] * 5,
        out_specs=pl.BlockSpec(memory_space=pltpu.VMEM),
        scratch_shapes=[
            pltpu.VMEM((steps, rows, det // PIECES), jnp.bfloat16),
            pltpu.VMEM((steps, rows, det // PIECES), jnp.bfloat16),
            pltpu.VMEM(table.shape, jnp.bfloat16),
            pltpu.SMEM((1, steps), jnp.int32),
            pltpu.SMEM((angles,), jnp.int32),
            pltpu.VMEM((2, det), jnp.bfloat16),
            pltpu.VMEM((2, chunks, LANES), jnp.float32),
            pltpu.VMEM((3, rows * chunks, LANES), jnp.float32),
            pltpu.VMEM((3, chunks, LANES), jnp.bfloat16),
            pltpu.VMEM((2, 3, chunks, LANES), jnp.bfloat16),
            pltpu.VMEM((2, 3, chunks, LANES), jnp.bfloat16),
            pltpu.VMEM((angles * 6, chunks, LANES), jnp.bfloat16),
            pltpu.VMEM((rows, 2, chunks, LANES), jnp.bfloat16),
            pltpu.VMEM((angles, 2, chunks, LANES), jnp.bfloat16),
            pltpu.VMEM((angles, chunks, LANES), jnp.float32),
            pltpu.VMEM((angles, chunks, LANES), jnp.float32),
            pltpu.VMEM((2 * chunks, angles, LANES), jnp.float32),
            pltpu.VMEM((6 * own * angles, WIDTH), jnp.float32),
            pltpu.SemaphoreType.DMA((1 + PIECES,)),
            pltpu.SemaphoreType.DMA,
            pltpu.SemaphoreType.DMA,
            pltpu.SemaphoreType.DMA((2,)),
            pltpu.SemaphoreType.REGULAR((GROUPS,)),
        ],
        compiler_params=pltpu.CompilerParams(
            collective_id=0, has_side_effects=True, vmem_limit_bytes=48 * 1024 * 1024
        ),
    )(*[pltpu.with_memory_space_constraint(x, pltpu.HBM) for x in (raw_frames, step_index, partner, flat_field[:, 0, :], table)])
    return result[:, None, :]


def solution(mesh):
    in_specs = (
        P("angle", None, "row", None),
        P("angle", None),
        P(),
        P(None, ("row", "angle"), None),
    )
    out_specs = P(None, ("row", "angle"), None)
    return jax.shard_map(local, mesh=mesh, in_specs=in_specs, out_specs=out_specs, check_vma=False)
```

```python
import math

import jax
import jax.numpy as jnp
import ml_dtypes
import numpy as np
from jax import lax
from jax.experimental import pallas as pl
from jax.experimental.pallas import tpu as pltpu
from jax.sharding import PartitionSpec as P

WIDTH = 256
LANES = 128
TILE = 8
PIECES = 2
SPLIT = 4
GROUPS = 2


def circulant_blocks(padlen):
    count = padlen // (2 * WIDTH)
    n = np.arange(padlen, dtype=np.float64)
    odd = np.arange(padlen) % 2 == 1
    taps = np.where(odd, (2.0 / padlen) / np.tan(np.pi * np.where(odd, n, 1.0) / padlen), 0.0)
    m = np.arange(count)[:, None, None]
    p = np.arange(WIDTH)[None, :, None]
    q = np.arange(WIDTH)[None, None, :]
    return taps[(2 * (WIDTH * m + q - p) - 1) % padlen].astype(ml_dtypes.bfloat16)


def loop(start, stop, body):
    if isinstance(start, int) and isinstance(stop, int) and stop - start <= 8:
        for i in range(start, stop):
            body(i)
    else:
        lax.fori_loop(start, stop, lambda i, _: body(i), None)


def aligned(value, step):
    return value if isinstance(value, int) else pl.multiple_of(value, step)


def kernel(
    angles, blocks_row, raw_hbm, step_hbm, partner_hbm, flat_hbm, table_hbm, out_ref,
    raw_first, raw_second, table, step_ref, partner_ref, flat_ref, flat_rows, corr, halo, partial, edge, both, smooth, recv, natural, mirrored, tiles, ring,
    halo_sem, recv_sem, ready, local_sem, send_sem,
):
    raw = (raw_first, raw_second)
    steps, rows, _ = raw_first.shape
    det = flat_ref.shape[1]
    chunks = det // LANES
    per = chunks // PIECES
    own = det // (2 * WIDTH)
    last = angles - 1
    me = lax.axis_index("angle")
    row = lax.axis_index("row")
    after = lax.rem(row + 1, blocks_row)
    before = lax.rem(row + blocks_row - 1, blocks_row)
    has_before = row > 0
    has_after = row < blocks_row - 1
    odd = lax.rem(row, 2) == 1
    even = jnp.logical_not(odd)
    cross_before = has_before & even
    cross_after = has_after & odd
    first_row = (me == 0) & cross_before
    last_row = (me == last) & cross_after
    merged = first_row | last_row

    final = jnp.where(me < angles // 2, last, 0)

    def landing(target):
        other = jnp.where(target < angles // 2, last, 0)
        return recv_sem.at[(me == other).astype(jnp.int32)]

    barrier = pltpu.get_barrier_semaphore()

    step_copy = pltpu.make_async_copy(step_hbm, step_ref, local_sem.at[0])
    step_copy.start()

    def raw_copy(p, part, parts):
        width = per * LANES // parts
        return pltpu.make_async_copy(
            raw_hbm.at[0, :, :, pl.ds(p * per * LANES + part * width, width)],
            raw[p].at[:, :, pl.ds(part * width, width)],
            local_sem.at[1 + p],
        )

    for p in range(PIECES):
        for part in range(SPLIT):
            raw_copy(p, part, SPLIT).start()

    def greet(a):
        pl.semaphore_signal(barrier, inc=1, device_id={"angle": a})

    loop(me + 1, angles, greet)

    @pl.when(even)
    def _():
        pl.semaphore_signal(barrier, inc=1, device_id={"row": after})

    @pl.when(odd)
    def _():
        pl.semaphore_signal(barrier, inc=1, device_id={"row": before})

    @pl.when(first_row)
    def _():
        loop(0, angles, lambda a: pl.semaphore_signal(
            barrier, inc=1, device_id={"angle": a, "row": before}
        ))

    @pl.when(last_row)
    def _():
        loop(0, angles, lambda a: pl.semaphore_signal(
            barrier, inc=1, device_id={"angle": a, "row": after}
        ))

    step_copy.wait()
    flat_copy = pltpu.make_async_copy(flat_hbm, flat_ref, local_sem.at[0])
    flat_copy.start()
    partner_copy = pltpu.make_async_copy(partner_hbm, partner_ref, local_sem.at[1])
    table_copy = pltpu.make_async_copy(table_hbm, table, local_sem.at[2])

    named = [step_ref[0, k] for k in range(steps)]
    frame_of = []
    for i in range(steps):
        at = jnp.int32(0)
        for k in range(1, steps):
            at = jnp.where(named[k] == i, jnp.int32(k), at)
        frame_of.append(at)
    assert steps == 8
    half_root = float(np.float32(math.sqrt(0.5)))

    def correlate(p, g):
        at = aligned(g * TILE, TILE)
        sums = [[], [], []]
        for c in range(per):
            f = [
                raw[p][frame_of[i], pl.ds(at, TILE), c * LANES : (c + 1) * LANES].astype(jnp.float32)
                for i in range(steps)
            ]
            less = [f[i] - f[i + 4] for i in range(4)]
            more = [f[i] + f[i + 4] for i in range(4)]
            sums[0].append(less[0] + (less[1] - less[3]) * half_root)
            sums[1].append(less[2] + (less[1] + less[3]) * half_root)
            sums[2].append((more[0] + more[2]) + (more[1] + more[3]))
        for q in range(3):
            turned = jnp.swapaxes(jnp.stack(sums[q]), 0, 1)
            for j in range(TILE):
                corr[q, pl.ds(aligned((at + j) * chunks + p * per, TILE), per), :] = turned[j]

    def line(p, q, i):
        return corr[q, pl.ds(aligned(i * chunks + p * per, TILE), per), :]

    def part_of(p):
        return slice(p * per, (p + 1) * per)

    def ratios(p, i, values):
        values = [v.astype(jnp.bfloat16).astype(jnp.float32) for v in values]
        scale = steps / values[2]
        for q in range(2):
            smooth[i, q, part_of(p), :] = (values[q] * scale).astype(jnp.bfloat16)

    def interior(p, i):
        ratios(p, i, [
            0.25 * line(p, q, i - 1) + 0.5 * line(p, q, i) + 0.25 * line(p, q, i + 1) for q in range(3)
        ])

    def border(p, side):
        at, inside = ((0, 1), (rows - 1, rows - 2))[side]
        inner = [0.5 * line(p, q, at) + 0.25 * line(p, q, inside) for q in range(3)]
        for q in range(3):
            partial[side, q, part_of(p), :] = inner[q].astype(jnp.bfloat16)
        ratios(p, at, inner)

    def rim(p, side):
        for q in range(3):
            edge[side, q, part_of(p), :] = (0.25 * line(p, q, (rows - 1, 0)[side])).astype(jnp.bfloat16)

    def joined(side):
        at, inside = ((0, 1), (rows - 1, rows - 2))[side]
        for p in range(PIECES):
            ratios(p, at, [
                halo[q, part_of(p), :].astype(jnp.float32) + 0.5 * line(p, q, at) + 0.25 * line(p, q, inside)
                for q in range(3)
            ])

    def halo_copy(side):
        return pltpu.make_async_remote_copy(
            src_ref=edge.at[side],
            dst_ref=halo,
            send_sem=send_sem,
            recv_sem=halo_sem,
            device_id={"row": (after, before)[side]},
        )

    def row_copy(target):
        return pltpu.make_async_remote_copy(
            src_ref=smooth.at[target],
            dst_ref=recv.at[me],
            send_sem=send_sem,
            recv_sem=landing(target),
            device_id={"angle": target},
        )

    def part_copy(side):
        return pltpu.make_async_remote_copy(
            src_ref=partial.at[side],
            dst_ref=both.at[pl.ds(me * 6, 3)],
            send_sem=send_sem,
            recv_sem=landing((0, last)[side]),
            device_id={"angle": (0, last)[side]},
        )

    def edge_copy(side):
        return pltpu.make_async_remote_copy(
            src_ref=edge.at[side],
            dst_ref=both.at[pl.ds(me * 6 + 3, 3)],
            send_sem=send_sem,
            recv_sem=landing((0, last)[side]),
            device_id=({"angle": 0, "row": after}, {"angle": last, "row": before})[side],
        )

    crossing = (cross_before, cross_after)
    outward = (cross_after, cross_before)

    def border_copies(side):
        target = (0, last)[side]

        @pl.when(crossing[side] & (me != target))
        def _():
            part_copy(side).start()

        @pl.when(jnp.logical_not(crossing[side]) & (me != target))
        def _():
            row_copy(target).start()

    def edge_start(side):
        @pl.when(outward[side])
        def _():
            edge_copy(side).start()

    reach = angles // GROUPS

    def tell(a):
        pl.semaphore_signal(ready.at[me // reach], inc=1, device_id={"angle": a})


    for p in range(PIECES):
        raw_copy(p, 0, 1).wait()
        (partner_copy, table_copy)[p].start()
        loop(0, rows // TILE, lambda g: correlate(p, g))

    for p in range(PIECES):
        border(p, 0)
        rim(p, 0)

    pl.semaphore_wait(barrier, me + has_before.astype(jnp.int32) + has_after.astype(jnp.int32))

    @pl.when(even)
    def _():
        border_copies(0)
        halo_copy(0).start()

    @pl.when(odd)
    def _():
        edge_start(0)

    loop(0, me, tell)
    for p in range(PIECES):
        loop(1, rows - 1, lambda i: interior(p, i))
        border(p, 1)
        rim(p, 1)

    @pl.when(odd)
    def _():
        halo_copy(1).start()

    def bulk():
        loop(1, jnp.minimum(me, last), lambda t: row_copy(t).start())

    @pl.when(even)
    def _():
        bulk()
        edge_start(1)

    @pl.when(odd)
    def _():
        halo_copy(0).wait_recv()
        joined(0)
        border_copies(0)
        bulk()

    @pl.when(even)
    def _():
        halo_copy(1).wait_recv()
        joined(1)

    for group in range(GROUPS):
        low, high = jnp.maximum(me + 1, group * reach), (group + 1) * reach

        @pl.when(low < high)
        def _():
            pl.semaphore_wait(ready.at[group], high - low)
            loop(low, min(high, last), lambda t: row_copy(t).start())

    border_copies(1)

    flat_copy.wait()
    for q in range(2):
        for c in range(chunks):
            flat_rows[q, c : c + 1, :] = flat_ref[q : q + 1, c * LANES : (c + 1) * LANES].astype(jnp.float32)
    partner_copy.wait()
    table_copy.wait()

    @pl.when(jnp.logical_not(merged))
    def _():
        recv[me] = smooth[me]

    @pl.when(first_row)
    def _():
        both[pl.ds(me * 6, 3)] = partial[0]

    @pl.when(last_row)
    def _():
        both[pl.ds(me * 6, 3)] = partial[1]

    lane = lax.broadcasted_iota(jnp.int32, (TILE, LANES), 1)
    sublane = lax.broadcasted_iota(jnp.int32, (TILE, LANES), 0)
    middle = LANES // 2
    lower = lane < middle
    paired = 2 * jnp.where(lower, lane, lane - middle)
    odd_first = lower == (lax.rem(sublane, 2) == 0)
    onward = paired + odd_first.astype(jnp.int32)
    backward = LANES - 2 - paired + odd_first.astype(jnp.int32)

    def landed(at, units):
        pltpu.make_async_remote_copy(
            src_ref=both.at[pl.ds(0, units)], dst_ref=both.at[pl.ds(0, units)],
            send_sem=send_sem, recv_sem=recv_sem.at[at], device_id={"row": after},
        ).wait_recv()

    def merge(a):
        values = [both[a * 6 + q].astype(jnp.float32) + both[a * 6 + 3 + q].astype(jnp.float32) for q in range(3)]
        scale = steps / values[2]
        for q in range(2):
            recv[a, q] = (values[q] * scale).astype(jnp.bfloat16)

    def differ(a):
        sine, cosine = recv[a, 1].astype(jnp.float32), recv[a, 0].astype(jnp.float32)
        value = sine * flat_rows[0] - cosine * flat_rows[1]
        dpc = value.astype(jnp.bfloat16).astype(jnp.float32)
        for c in range(0, chunks, TILE):
            natural[a, c : c + TILE, :] = jnp.take_along_axis(dpc[c : c + TILE], onward, axis=1)
            mirrored[a, c : c + TILE, :] = -jnp.take_along_axis(dpc[c : c + TILE], backward, axis=1)

    def others(body):
        loop(0, last, lambda k: body(lax.rem(final + 1 + k, angles)))

    @pl.when(merged)
    def _():
        landed(0, 6 * (angles - 2) + 3)
        others(merge)

    @pl.when(jnp.logical_not(merged))
    def _():
        landed(0, 2 * (angles - 2))

    others(differ)
    natural[final] = jnp.zeros(natural.shape[1:], natural.dtype)
    mirrored[final] = jnp.zeros(mirrored.shape[1:], mirrored.dtype)

    def turn(g):
        base = aligned(g * TILE, TILE)
        for c in range(0, chunks, TILE):
            here = jnp.swapaxes(jnp.stack([natural[base + j, c : c + TILE, :] for j in range(TILE)]), 0, 1)
            there = jnp.swapaxes(
                jnp.stack([mirrored[partner_ref[base + j], c : c + TILE, :] for j in range(TILE)]), 0, 1
            )
            for j in range(TILE):
                tiles[chunks + c + j, pl.ds(base, TILE), :] = here[j]
                tiles[chunks - 1 - c - j, pl.ds(base, TILE), :] = there[j]

    loop(0, angles // TILE, turn)

    @pl.when(merged)
    def _():
        landed(1, 6)
        merge(final)

    @pl.when(jnp.logical_not(merged))
    def _():
        landed(1, 2)

    differ(final)

    def place(g):
        base = aligned(g * TILE, TILE)
        here, there = sublane + base == final, sublane + base == partner_ref[final]

        def tile(c):
            if c < chunks:
                row = mirrored[final, chunks - 1 - c : chunks - c, :]
                return jnp.where(there, row, tiles[c, pl.ds(base, TILE), :])
            row = natural[final, c - chunks : c - chunks + 1, :]
            return jnp.where(here, row, tiles[c, pl.ds(base, TILE), :])

        uneven, turned = [], []
        for block in range(chunks):
            first, second = tile(2 * block), tile(2 * block + 1)
            uneven.append(jnp.where(lower, first, second))
            turned.append(pltpu.roll(jnp.where(lower, second, first), middle - 1, 1))
        for block in range(chunks):
            shifted = jnp.where(lane < LANES - 1, turned[block], turned[(block + 1) % chunks])
            group, half = divmod(block, 2)
            lanes = slice(half * LANES, (half + 1) * LANES)
            for k in (group, group + 2 * own)[: 2 if group < own else 1]:
                ring[pl.ds(2 * k * angles + base, TILE), lanes] = uneven[block]
                ring[pl.ds((2 * k + 1) * angles + base, TILE), lanes] = shifted

    loop(0, angles // TILE, place)

    turns = 2 * own
    height = 2 * own * angles
    total = jnp.zeros((height, WIDTH), jnp.float32)
    for m in range(turns):
        first = ((own - m) % turns) * 2 * angles
        window = ring[first : first + height].astype(jnp.bfloat16)
        total = total + jnp.dot(window, table[m], preferred_element_type=jnp.float32)
    total = total.astype(jnp.bfloat16).astype(jnp.float32)
    second_half = lane // 2 + middle
    for k in range(own):
        for half in range(2):
            lanes = slice(half * LANES, (half + 1) * LANES)
            for base in range(0, angles, TILE):
                at = 2 * k * angles + base
                even_at = total[at : at + TILE, lanes]
                odd_at = total[at + angles : at + angles + TILE, lanes]
                for part, index in enumerate((lane // 2, second_half)):
                    c = 4 * k + 2 * half + part
                    mixed = jnp.where(
                        lax.rem(lane, 2) == 0,
                        jnp.take_along_axis(even_at, index, axis=1),
                        jnp.take_along_axis(odd_at, index, axis=1),
                    )
                    out_ref[base : base + TILE, c * LANES : (c + 1) * LANES] = mixed.astype(jnp.bfloat16)

    crossed = cross_before | cross_after

    def sent(units):
        pltpu.make_async_remote_copy(
            src_ref=both.at[pl.ds(0, units)], dst_ref=both.at[pl.ds(0, units)],
            send_sem=send_sem, recv_sem=halo_sem, device_id={"row": after},
        ).wait_send()

    @pl.when(jnp.logical_not(crossed))
    def _():
        sent(2 * angles + 1)

    @pl.when(crossed & jnp.logical_not(merged))
    def _():
        sent(2 * angles + 5)

    @pl.when(merged)
    def _():
        sent(2 * angles + 4)


def local(raw_frames, step_index, partner, flat_field):
    _, steps, rows, det = raw_frames.shape
    angles = lax.axis_size("angle")
    blocks_row = lax.axis_size("row")
    chunks = det // LANES
    own = det // (2 * WIDTH)
    assert rows == angles and rows % TILE == 0 and blocks_row % 2 == 0 and angles % GROUPS == 0 and raw_frames.shape[0] == 1
    table = jnp.asarray(circulant_blocks(2 * det))

    def body(*refs):
        pl.run_scoped(
            lambda *own_sems: kernel(angles, blocks_row, *refs, *own_sems),
            pltpu.SemaphoreType.DMA((1 + PIECES,)),
            pltpu.SemaphoreType.DMA,
        )

    result = pl.pallas_call(
        body,
        out_shape=jax.ShapeDtypeStruct((angles, det), jnp.bfloat16),
        in_specs=[pl.BlockSpec(memory_space=pltpu.HBM)] * 5,
        out_specs=pl.BlockSpec(memory_space=pltpu.VMEM),
        scratch_shapes=[
            pltpu.VMEM((steps, rows, det // PIECES), jnp.bfloat16),
            pltpu.VMEM((steps, rows, det // PIECES), jnp.bfloat16),
            pltpu.VMEM(table.shape, jnp.bfloat16),
            pltpu.SMEM((1, steps), jnp.int32),
            pltpu.SMEM((angles,), jnp.int32),
            pltpu.VMEM((2, det), jnp.bfloat16),
            pltpu.VMEM((2, chunks, LANES), jnp.float32),
            pltpu.VMEM((3, rows * chunks, LANES), jnp.float32),
            pltpu.VMEM((3, chunks, LANES), jnp.bfloat16),
            pltpu.VMEM((2, 3, chunks, LANES), jnp.bfloat16),
            pltpu.VMEM((2, 3, chunks, LANES), jnp.bfloat16),
            pltpu.VMEM((angles * 6, chunks, LANES), jnp.bfloat16),
            pltpu.VMEM((rows, 2, chunks, LANES), jnp.bfloat16),
            pltpu.VMEM((angles, 2, chunks, LANES), jnp.bfloat16),
            pltpu.VMEM((angles, chunks, LANES), jnp.float32),
            pltpu.VMEM((angles, chunks, LANES), jnp.float32),
            pltpu.VMEM((2 * chunks, angles, LANES), jnp.float32),
            pltpu.VMEM((6 * own * angles, WIDTH), jnp.float32),
            pltpu.SemaphoreType.DMA,
            pltpu.SemaphoreType.DMA((2,)),
            pltpu.SemaphoreType.REGULAR((GROUPS,)),
        ],
        compiler_params=pltpu.CompilerParams(
            collective_id=0, has_side_effects=True, vmem_limit_bytes=48 * 1024 * 1024
        ),
    )(*[pltpu.with_memory_space_constraint(x, pltpu.HBM) for x in (raw_frames, step_index, partner, flat_field[:, 0, :], table)])
    return result[:, None, :]


def solution(mesh):
    in_specs = (
        P("angle", None, "row", None),
        P("angle", None),
        P(),
        P(None, ("row", "angle"), None),
    )
    out_specs = P(None, ("row", "angle"), None)
    return jax.shard_map(local, mesh=mesh, in_specs=in_specs, out_specs=out_specs, check_vma=False)
```

```python
import math

import jax
import jax.numpy as jnp
import ml_dtypes
import numpy as np
from jax import lax
from jax.experimental import pallas as pl
from jax.experimental.pallas import tpu as pltpu
from jax.sharding import PartitionSpec as P

WIDTH = 256
LANES = 128
TILE = 8
PIECES = 2
PARTS = 2
SPLIT = 2
GROUPS = 2


def circulant_blocks(padlen):
    count = padlen // (2 * WIDTH)
    n = np.arange(padlen, dtype=np.float64)
    odd = np.arange(padlen) % 2 == 1
    taps = np.where(odd, (2.0 / padlen) / np.tan(np.pi * np.where(odd, n, 1.0) / padlen), 0.0)
    m = np.arange(count)[:, None, None]
    p = np.arange(WIDTH)[None, :, None]
    q = np.arange(WIDTH)[None, None, :]
    return taps[(2 * (WIDTH * m + q - p) - 1) % padlen].astype(ml_dtypes.bfloat16)


def loop(start, stop, body):
    if isinstance(start, int) and isinstance(stop, int) and stop - start <= 8:
        for i in range(start, stop):
            body(i)
    else:
        lax.fori_loop(start, stop, lambda i, _: body(i), None)


def aligned(value, step):
    return value if isinstance(value, int) else pl.multiple_of(value, step)


def kernel(
    angles, blocks_row, raw_hbm, step_hbm, partner_hbm, flat_hbm, table_hbm, out_ref,
    raw_0, raw_1, raw_2, raw_3, table, step_ref, partner_ref, flat_ref, flat_rows, corr, halo, partial, edge, both, smooth, recv, natural, mirrored, tiles, ring,
    halo_sem, recv_sem, ready, local_sem, send_sem,
):
    raw = (raw_0, raw_1, raw_2, raw_3)
    steps, rows, _ = raw_0.shape
    det = flat_ref.shape[1]
    chunks = det // LANES
    per = chunks // PIECES
    own = det // (2 * WIDTH)
    last = angles - 1
    me = lax.axis_index("angle")
    row = lax.axis_index("row")
    after = lax.rem(row + 1, blocks_row)
    before = lax.rem(row + blocks_row - 1, blocks_row)
    has_before = row > 0
    has_after = row < blocks_row - 1
    odd = lax.rem(row, 2) == 1
    even = jnp.logical_not(odd)
    cross_before = has_before & even
    cross_after = has_after & odd
    first_row = (me == 0) & cross_before
    last_row = (me == last) & cross_after
    merged = first_row | last_row

    final = jnp.where(me < angles // 2, last, 0)

    def landing(target):
        other = jnp.where(target < angles // 2, last, 0)
        return recv_sem.at[(me == other).astype(jnp.int32)]

    barrier = pltpu.get_barrier_semaphore()

    step_copy = pltpu.make_async_copy(step_hbm, step_ref, local_sem.at[0])
    step_copy.start()

    def raw_copy(b, part, parts):
        width = raw_0.shape[2] // parts
        return pltpu.make_async_copy(
            raw_hbm.at[0, :, :, pl.ds(b * raw_0.shape[2] + part * width, width)],
            raw[b].at[:, :, pl.ds(part * width, width)],
            local_sem.at[3 + b],
        )

    for b in range(PIECES * PARTS):
        for part in range(SPLIT):
            raw_copy(b, part, SPLIT).start()

    def greet(a):
        pl.semaphore_signal(barrier, inc=1, device_id={"angle": a})

    loop(me + 1, angles, greet)

    @pl.when(even)
    def _():
        pl.semaphore_signal(barrier, inc=1, device_id={"row": after})

    @pl.when(odd)
    def _():
        pl.semaphore_signal(barrier, inc=1, device_id={"row": before})

    @pl.when(first_row)
    def _():
        loop(0, angles, lambda a: pl.semaphore_signal(
            barrier, inc=1, device_id={"angle": a, "row": before}
        ))

    @pl.when(last_row)
    def _():
        loop(0, angles, lambda a: pl.semaphore_signal(
            barrier, inc=1, device_id={"angle": a, "row": after}
        ))

    step_copy.wait()
    flat_copy = pltpu.make_async_copy(flat_hbm, flat_ref, local_sem.at[0])
    flat_copy.start()
    partner_copy = pltpu.make_async_copy(partner_hbm, partner_ref, local_sem.at[1])
    table_copy = pltpu.make_async_copy(table_hbm, table, local_sem.at[2])

    named = [step_ref[0, k] for k in range(steps)]
    frame_of = []
    for i in range(steps):
        at = jnp.int32(0)
        for k in range(1, steps):
            at = jnp.where(named[k] == i, jnp.int32(k), at)
        frame_of.append(at)
    assert steps == 8
    half_root = float(np.float32(math.sqrt(0.5)))

    def correlate(p, g):
        at = aligned(g * TILE, TILE)
        sums = [[], [], []]
        for c in range(per):
            b, c = p * PARTS + c // (per // PARTS), c % (per // PARTS)
            if rows == TILE and c == 0:
                raw_copy(b, 0, 1).wait()
            f = [
                raw[b][frame_of[i], pl.ds(at, TILE), c * LANES : (c + 1) * LANES].astype(jnp.float32)
                for i in range(steps)
            ]
            less = [f[i] - f[i + 4] for i in range(4)]
            more = [f[i] + f[i + 4] for i in range(4)]
            sums[0].append(less[0] + (less[1] - less[3]) * half_root)
            sums[1].append(less[2] + (less[1] + less[3]) * half_root)
            sums[2].append((more[0] + more[2]) + (more[1] + more[3]))
        for q in range(3):
            turned = jnp.swapaxes(jnp.stack(sums[q]), 0, 1)
            for j in range(TILE):
                corr[q, pl.ds(aligned((at + j) * chunks + p * per, TILE), per), :] = turned[j]

    def line(p, q, i):
        return corr[q, pl.ds(aligned(i * chunks + p * per, TILE), per), :]

    def part_of(p):
        return slice(p * per, (p + 1) * per)

    def ratios(p, i, values):
        values = [v.astype(jnp.bfloat16).astype(jnp.float32) for v in values]
        scale = steps / values[2]
        for q in range(2):
            smooth[i, q, part_of(p), :] = (values[q] * scale).astype(jnp.bfloat16)

    def interior(p, i):
        ratios(p, i, [
            0.25 * line(p, q, i - 1) + 0.5 * line(p, q, i) + 0.25 * line(p, q, i + 1) for q in range(3)
        ])

    def border(p, side):
        at, inside = ((0, 1), (rows - 1, rows - 2))[side]
        inner = [0.5 * line(p, q, at) + 0.25 * line(p, q, inside) for q in range(3)]
        for q in range(3):
            partial[side, q, part_of(p), :] = inner[q].astype(jnp.bfloat16)
        ratios(p, at, inner)

    def rim(p, side):
        for q in range(3):
            edge[side, q, part_of(p), :] = (0.25 * line(p, q, (rows - 1, 0)[side])).astype(jnp.bfloat16)

    def joined(side):
        at, inside = ((0, 1), (rows - 1, rows - 2))[side]
        for p in range(PIECES):
            ratios(p, at, [
                halo[q, part_of(p), :].astype(jnp.float32) + 0.5 * line(p, q, at) + 0.25 * line(p, q, inside)
                for q in range(3)
            ])

    def halo_copy(side):
        return pltpu.make_async_remote_copy(
            src_ref=edge.at[side],
            dst_ref=halo,
            send_sem=send_sem,
            recv_sem=halo_sem,
            device_id={"row": (after, before)[side]},
        )

    def row_copy(target):
        return pltpu.make_async_remote_copy(
            src_ref=smooth.at[target],
            dst_ref=recv.at[me],
            send_sem=send_sem,
            recv_sem=landing(target),
            device_id={"angle": target},
        )

    def part_copy(side):
        return pltpu.make_async_remote_copy(
            src_ref=partial.at[side],
            dst_ref=both.at[pl.ds(me * 6, 3)],
            send_sem=send_sem,
            recv_sem=landing((0, last)[side]),
            device_id={"angle": (0, last)[side]},
        )

    def edge_copy(side):
        return pltpu.make_async_remote_copy(
            src_ref=edge.at[side],
            dst_ref=both.at[pl.ds(me * 6 + 3, 3)],
            send_sem=send_sem,
            recv_sem=landing((0, last)[side]),
            device_id=({"angle": 0, "row": after}, {"angle": last, "row": before})[side],
        )

    crossing = (cross_before, cross_after)
    outward = (cross_after, cross_before)

    def border_copies(side):
        target = (0, last)[side]

        @pl.when(crossing[side] & (me != target))
        def _():
            part_copy(side).start()

        @pl.when(jnp.logical_not(crossing[side]) & (me != target))
        def _():
            row_copy(target).start()

    def edge_start(side):
        @pl.when(outward[side])
        def _():
            edge_copy(side).start()

    reach = angles // GROUPS

    def tell(a):
        pl.semaphore_signal(ready.at[me // reach], inc=1, device_id={"angle": a})


    for p in range(PIECES):
        for b in range(p * PARTS, (p + 1) * PARTS) if rows > TILE else ():
            raw_copy(b, 0, 1).wait()
        loop(0, rows // TILE, lambda g: correlate(p, g))
        border(p, 0)
        rim(p, 0)

    partner_copy.start()
    table_copy.start()

    pl.semaphore_wait(barrier, me + has_before.astype(jnp.int32) + has_after.astype(jnp.int32))

    @pl.when(even)
    def _():
        border_copies(0)
        halo_copy(0).start()

    @pl.when(odd)
    def _():
        edge_start(0)

    loop(0, me, tell)
    for p in range(PIECES):
        loop(1, rows - 1, lambda i: interior(p, i))
        border(p, 1)
        rim(p, 1)

    @pl.when(odd)
    def _():
        halo_copy(1).start()

    def bulk():
        loop(1, jnp.minimum(me, last), lambda t: row_copy(t).start())

    @pl.when(even)
    def _():
        bulk()
        edge_start(1)

    @pl.when(odd)
    def _():
        halo_copy(0).wait_recv()
        joined(0)
        border_copies(0)
        bulk()

    @pl.when(even)
    def _():
        halo_copy(1).wait_recv()
        joined(1)

    for group in range(GROUPS):
        low, high = jnp.maximum(me + 1, group * reach), (group + 1) * reach

        @pl.when(low < high)
        def _():
            pl.semaphore_wait(ready.at[group], high - low)
            loop(low, min(high, last), lambda t: row_copy(t).start())

    border_copies(1)

    flat_copy.wait()
    for q in range(2):
        for c in range(chunks):
            flat_rows[q, c : c + 1, :] = flat_ref[q : q + 1, c * LANES : (c + 1) * LANES].astype(jnp.float32)
    partner_copy.wait()
    table_copy.wait()

    @pl.when(jnp.logical_not(merged))
    def _():
        recv[me] = smooth[me]

    @pl.when(first_row)
    def _():
        both[pl.ds(me * 6, 3)] = partial[0]

    @pl.when(last_row)
    def _():
        both[pl.ds(me * 6, 3)] = partial[1]

    lane = lax.broadcasted_iota(jnp.int32, (TILE, LANES), 1)
    sublane = lax.broadcasted_iota(jnp.int32, (TILE, LANES), 0)
    middle = LANES // 2
    lower = lane < middle
    paired = 2 * jnp.where(lower, lane, lane - middle)
    odd_first = lower == (lax.rem(sublane, 2) == 0)
    onward = paired + odd_first.astype(jnp.int32)
    backward = LANES - 2 - paired + odd_first.astype(jnp.int32)

    def landed(at, units):
        pltpu.make_async_remote_copy(
            src_ref=both.at[pl.ds(0, units)], dst_ref=both.at[pl.ds(0, units)],
            send_sem=send_sem, recv_sem=recv_sem.at[at], device_id={"row": after},
        ).wait_recv()

    def merge(a):
        values = [both[a * 6 + q].astype(jnp.float32) + both[a * 6 + 3 + q].astype(jnp.float32) for q in range(3)]
        scale = steps / values[2]
        for q in range(2):
            recv[a, q] = (values[q] * scale).astype(jnp.bfloat16)

    def differ(a):
        sine, cosine = recv[a, 1].astype(jnp.float32), recv[a, 0].astype(jnp.float32)
        value = sine * flat_rows[0] - cosine * flat_rows[1]
        dpc = value.astype(jnp.bfloat16).astype(jnp.float32)
        for c in range(0, chunks, TILE):
            natural[a, c : c + TILE, :] = jnp.take_along_axis(dpc[c : c + TILE], onward, axis=1)
            mirrored[a, c : c + TILE, :] = -jnp.take_along_axis(dpc[c : c + TILE], backward, axis=1)

    def others(body):
        loop(0, last, lambda k: body(lax.rem(final + 1 + k, angles)))

    @pl.when(merged)
    def _():
        landed(0, 6 * (angles - 2) + 3)
        others(merge)

    @pl.when(jnp.logical_not(merged))
    def _():
        landed(0, 2 * (angles - 2))

    others(differ)
    natural[final] = jnp.zeros(natural.shape[1:], natural.dtype)
    mirrored[final] = jnp.zeros(mirrored.shape[1:], mirrored.dtype)

    def turn(g):
        base = aligned(g * TILE, TILE)
        for c in range(0, chunks, TILE):
            here = jnp.swapaxes(jnp.stack([natural[base + j, c : c + TILE, :] for j in range(TILE)]), 0, 1)
            there = jnp.swapaxes(
                jnp.stack([mirrored[partner_ref[base + j], c : c + TILE, :] for j in range(TILE)]), 0, 1
            )
            for j in range(TILE):
                tiles[chunks + c + j, pl.ds(base, TILE), :] = here[j]
                tiles[chunks - 1 - c - j, pl.ds(base, TILE), :] = there[j]

    loop(0, angles // TILE, turn)

    @pl.when(merged)
    def _():
        landed(1, 6)
        merge(final)

    @pl.when(jnp.logical_not(merged))
    def _():
        landed(1, 2)

    differ(final)

    def place(g):
        base = aligned(g * TILE, TILE)
        here, there = sublane + base == final, sublane + base == partner_ref[final]

        def tile(c):
            if c < chunks:
                row = mirrored[final, chunks - 1 - c : chunks - c, :]
                return jnp.where(there, row, tiles[c, pl.ds(base, TILE), :])
            row = natural[final, c - chunks : c - chunks + 1, :]
            return jnp.where(here, row, tiles[c, pl.ds(base, TILE), :])

        uneven, turned = [], []
        for block in range(chunks):
            first, second = tile(2 * block), tile(2 * block + 1)
            uneven.append(jnp.where(lower, first, second))
            turned.append(pltpu.roll(jnp.where(lower, second, first), middle - 1, 1))
        for block in range(chunks):
            shifted = jnp.where(lane < LANES - 1, turned[block], turned[(block + 1) % chunks])
            group, half = divmod(block, 2)
            lanes = slice(half * LANES, (half + 1) * LANES)
            for k in (group, group + 2 * own)[: 2 if group < own else 1]:
                ring[pl.ds(2 * k * angles + base, TILE), lanes] = uneven[block]
                ring[pl.ds((2 * k + 1) * angles + base, TILE), lanes] = shifted

    loop(0, angles // TILE, place)

    turns = 2 * own
    height = 2 * own * angles
    total = jnp.zeros((height, WIDTH), jnp.float32)
    for m in range(turns):
        first = ((own - m) % turns) * 2 * angles
        window = ring[first : first + height].astype(jnp.bfloat16)
        total = total + jnp.dot(window, table[m], preferred_element_type=jnp.float32)
    total = total.astype(jnp.bfloat16).astype(jnp.float32)
    second_half = lane // 2 + middle
    for k in range(own):
        for half in range(2):
            lanes = slice(half * LANES, (half + 1) * LANES)
            for base in range(0, angles, TILE):
                at = 2 * k * angles + base
                even_at = total[at : at + TILE, lanes]
                odd_at = total[at + angles : at + angles + TILE, lanes]
                for part, index in enumerate((lane // 2, second_half)):
                    c = 4 * k + 2 * half + part
                    mixed = jnp.where(
                        lax.rem(lane, 2) == 0,
                        jnp.take_along_axis(even_at, index, axis=1),
                        jnp.take_along_axis(odd_at, index, axis=1),
                    )
                    out_ref[base : base + TILE, c * LANES : (c + 1) * LANES] = mixed.astype(jnp.bfloat16)

    crossed = cross_before | cross_after

    def sent(units):
        pltpu.make_async_remote_copy(
            src_ref=both.at[pl.ds(0, units)], dst_ref=both.at[pl.ds(0, units)],
            send_sem=send_sem, recv_sem=halo_sem, device_id={"row": after},
        ).wait_send()

    @pl.when(jnp.logical_not(crossed))
    def _():
        sent(2 * angles + 1)

    @pl.when(crossed & jnp.logical_not(merged))
    def _():
        sent(2 * angles + 5)

    @pl.when(merged)
    def _():
        sent(2 * angles + 4)


def local(raw_frames, step_index, partner, flat_field):
    _, steps, rows, det = raw_frames.shape
    angles = lax.axis_size("angle")
    blocks_row = lax.axis_size("row")
    chunks = det // LANES
    own = det // (2 * WIDTH)
    assert rows == angles and rows % TILE == 0 and blocks_row % 2 == 0 and angles % GROUPS == 0 and raw_frames.shape[0] == 1
    table = jnp.asarray(circulant_blocks(2 * det))

    def body(*refs):
        pl.run_scoped(
            lambda *own_sems: kernel(angles, blocks_row, *refs, *own_sems),
            pltpu.SemaphoreType.DMA((3 + PIECES * PARTS,)),
            pltpu.SemaphoreType.DMA,
        )

    result = pl.pallas_call(
        body,
        out_shape=jax.ShapeDtypeStruct((angles, det), jnp.bfloat16),
        in_specs=[pl.BlockSpec(memory_space=pltpu.HBM)] * 5,
        out_specs=pl.BlockSpec(memory_space=pltpu.VMEM),
        scratch_shapes=[
            *[pltpu.VMEM((steps, rows, det // (PIECES * PARTS)), jnp.bfloat16)] * (PIECES * PARTS),
            pltpu.VMEM(table.shape, jnp.bfloat16),
            pltpu.SMEM((1, steps), jnp.int32),
            pltpu.SMEM((angles,), jnp.int32),
            pltpu.VMEM((2, det), jnp.bfloat16),
            pltpu.VMEM((2, chunks, LANES), jnp.float32),
            pltpu.VMEM((3, rows * chunks, LANES), jnp.float32),
            pltpu.VMEM((3, chunks, LANES), jnp.bfloat16),
            pltpu.VMEM((2, 3, chunks, LANES), jnp.bfloat16),
            pltpu.VMEM((2, 3, chunks, LANES), jnp.bfloat16),
            pltpu.VMEM((angles * 6, chunks, LANES), jnp.bfloat16),
            pltpu.VMEM((rows, 2, chunks, LANES), jnp.bfloat16),
            pltpu.VMEM((angles, 2, chunks, LANES), jnp.bfloat16),
            pltpu.VMEM((angles, chunks, LANES), jnp.float32),
            pltpu.VMEM((angles, chunks, LANES), jnp.float32),
            pltpu.VMEM((2 * chunks, angles, LANES), jnp.float32),
            pltpu.VMEM((6 * own * angles, WIDTH), jnp.float32),
            pltpu.SemaphoreType.DMA,
            pltpu.SemaphoreType.DMA((2,)),
            pltpu.SemaphoreType.REGULAR((GROUPS,)),
        ],
        compiler_params=pltpu.CompilerParams(
            collective_id=0, has_side_effects=True, vmem_limit_bytes=48 * 1024 * 1024
        ),
    )(*[pltpu.with_memory_space_constraint(x, pltpu.HBM) for x in (raw_frames, step_index, partner, flat_field[:, 0, :], table)])
    return result[:, None, :]


def solution(mesh):
    in_specs = (
        P("angle", None, "row", None),
        P("angle", None),
        P(),
        P(None, ("row", "angle"), None),
    )
    out_specs = P(None, ("row", "angle"), None)
    return jax.shard_map(local, mesh=mesh, in_specs=in_specs, out_specs=out_specs, check_vma=False)
```

```python
import math

import jax
import jax.numpy as jnp
import ml_dtypes
import numpy as np
from jax import lax
from jax.experimental import pallas as pl
from jax.experimental.pallas import tpu as pltpu
from jax.sharding import PartitionSpec as P

WIDTH = 256
LANES = 128
TILE = 8
PIECES = 2
PARTS = 2
SPLIT = 2
GROUPS = 2


def circulant_blocks(padlen):
    count = padlen // (2 * WIDTH)
    n = np.arange(padlen, dtype=np.float64)
    odd = np.arange(padlen) % 2 == 1
    taps = np.where(odd, (2.0 / padlen) / np.tan(np.pi * np.where(odd, n, 1.0) / padlen), 0.0)
    m = np.arange(count)[:, None, None]
    p = np.arange(WIDTH)[None, :, None]
    q = np.arange(WIDTH)[None, None, :]
    return taps[(2 * (WIDTH * m + q - p) - 1) % padlen].astype(ml_dtypes.bfloat16)


def loop(start, stop, body):
    if isinstance(start, int) and isinstance(stop, int) and stop - start <= 8:
        for i in range(start, stop):
            body(i)
    else:
        lax.fori_loop(start, stop, lambda i, _: body(i), None)


def aligned(value, step):
    return value if isinstance(value, int) else pl.multiple_of(value, step)


def kernel(
    angles, blocks_row, raw_hbm, step_hbm, partner_hbm, flat_hbm, table_hbm, out_ref,
    raw_0, raw_1, raw_2, raw_3, table, step_ref, partner_ref, flat_ref, flat_rows, corr, halo, partial, edge, both, smooth, recv, natural, mirrored, tiles, ring,
    halo_sem, recv_sem, ready, local_sem, send_sem,
):
    raw = (raw_0, raw_1, raw_2, raw_3)
    steps, rows, _ = raw_0.shape
    det = flat_ref.shape[1]
    chunks = det // LANES
    per = chunks // PIECES
    own = det // (2 * WIDTH)
    last = angles - 1
    me = lax.axis_index("angle")
    row = lax.axis_index("row")
    after = lax.rem(row + 1, blocks_row)
    before = lax.rem(row + blocks_row - 1, blocks_row)
    has_before = row > 0
    has_after = row < blocks_row - 1
    odd = lax.rem(row, 2) == 1
    even = jnp.logical_not(odd)
    cross_before = has_before & even
    cross_after = has_after & odd
    first_row = (me == 0) & cross_before
    last_row = (me == last) & cross_after
    merged = first_row | last_row

    final = jnp.where(me < angles // 2, last, 0)

    def landing(target):
        other = jnp.where(target < angles // 2, last, 0)
        return recv_sem.at[(me == other).astype(jnp.int32)]

    barrier = pltpu.get_barrier_semaphore()

    step_copy = pltpu.make_async_copy(step_hbm, step_ref, local_sem.at[0])
    step_copy.start()

    def raw_copy(b, part, parts):
        width = raw_0.shape[2] // parts
        return pltpu.make_async_copy(
            raw_hbm.at[0, :, :, pl.ds(b * raw_0.shape[2] + part * width, width)],
            raw[b].at[:, :, pl.ds(part * width, width)],
            local_sem.at[3 + b],
        )

    for b in range(PIECES * PARTS):
        for part in range(SPLIT):
            raw_copy(b, part, SPLIT).start()

    def greet(a):
        pl.semaphore_signal(barrier, inc=1, device_id={"angle": a})

    loop(0, last - me, lambda k: greet(last - k))

    @pl.when(even)
    def _():
        pl.semaphore_signal(barrier, inc=1, device_id={"row": after})

    @pl.when(odd)
    def _():
        pl.semaphore_signal(barrier, inc=1, device_id={"row": before})

    @pl.when(first_row)
    def _():
        loop(0, angles, lambda a: pl.semaphore_signal(
            barrier, inc=1, device_id={"angle": a, "row": before}
        ))

    @pl.when(last_row)
    def _():
        loop(0, angles, lambda a: pl.semaphore_signal(
            barrier, inc=1, device_id={"angle": a, "row": after}
        ))

    step_copy.wait()
    flat_copy = pltpu.make_async_copy(flat_hbm, flat_ref, local_sem.at[0])
    flat_copy.start()
    partner_copy = pltpu.make_async_copy(partner_hbm, partner_ref, local_sem.at[1])
    table_copy = pltpu.make_async_copy(table_hbm, table, local_sem.at[2])

    named = [step_ref[0, k] for k in range(steps)]
    frame_of = []
    for i in range(steps):
        at = jnp.int32(0)
        for k in range(1, steps):
            at = jnp.where(named[k] == i, jnp.int32(k), at)
        frame_of.append(at)
    assert steps == 8
    half_root = float(np.float32(math.sqrt(0.5)))

    def correlate(p, g):
        at = aligned(g * TILE, TILE)
        sums = [[], [], []]
        for c in range(per):
            b, c = p * PARTS + c // (per // PARTS), c % (per // PARTS)
            if rows == TILE and c == 0:
                raw_copy(b, 0, 1).wait()
            f = [
                raw[b][frame_of[i], pl.ds(at, TILE), c * LANES : (c + 1) * LANES].astype(jnp.float32)
                for i in range(steps)
            ]
            less = [f[i] - f[i + 4] for i in range(4)]
            more = [f[i] + f[i + 4] for i in range(4)]
            sums[0].append(less[0] + (less[1] - less[3]) * half_root)
            sums[1].append(less[2] + (less[1] + less[3]) * half_root)
            sums[2].append((more[0] + more[2]) + (more[1] + more[3]))
        for q in range(3):
            turned = jnp.swapaxes(jnp.stack(sums[q]), 0, 1)
            for j in range(TILE):
                corr[q, pl.ds(aligned((at + j) * chunks + p * per, TILE), per), :] = turned[j]

    def line(p, q, i):
        return corr[q, pl.ds(aligned(i * chunks + p * per, TILE), per), :]

    def part_of(p):
        return slice(p * per, (p + 1) * per)

    def ratios(p, i, values):
        values = [v.astype(jnp.bfloat16).astype(jnp.float32) for v in values]
        scale = 1.0 / values[2]
        for q in range(2):
            smooth[i, q, part_of(p), :] = (values[q] * scale).astype(jnp.bfloat16)

    def interior(p, i):
        ratios(p, i, [
            0.25 * line(p, q, i - 1) + 0.5 * line(p, q, i) + 0.25 * line(p, q, i + 1) for q in range(3)
        ])

    def border(p, side):
        at, inside = ((0, 1), (rows - 1, rows - 2))[side]
        inner = [0.5 * line(p, q, at) + 0.25 * line(p, q, inside) for q in range(3)]
        for q in range(3):
            partial[side, q, part_of(p), :] = inner[q].astype(jnp.bfloat16)
        ratios(p, at, inner)

    def rim(p, side):
        for q in range(3):
            edge[side, q, part_of(p), :] = (0.25 * line(p, q, (rows - 1, 0)[side])).astype(jnp.bfloat16)

    def joined(side):
        at, inside = ((0, 1), (rows - 1, rows - 2))[side]
        for p in range(PIECES):
            ratios(p, at, [
                halo[q, part_of(p), :].astype(jnp.float32) + 0.5 * line(p, q, at) + 0.25 * line(p, q, inside)
                for q in range(3)
            ])

    def halo_copy(side):
        return pltpu.make_async_remote_copy(
            src_ref=edge.at[side],
            dst_ref=halo,
            send_sem=send_sem,
            recv_sem=halo_sem,
            device_id={"row": (after, before)[side]},
        )

    def row_copy(target):
        return pltpu.make_async_remote_copy(
            src_ref=smooth.at[target],
            dst_ref=recv.at[me],
            send_sem=send_sem,
            recv_sem=landing(target),
            device_id={"angle": target},
        )

    def part_copy(side):
        return pltpu.make_async_remote_copy(
            src_ref=partial.at[side],
            dst_ref=both.at[pl.ds(me * 6, 3)],
            send_sem=send_sem,
            recv_sem=landing((0, last)[side]),
            device_id={"angle": (0, last)[side]},
        )

    def edge_copy(side):
        return pltpu.make_async_remote_copy(
            src_ref=edge.at[side],
            dst_ref=both.at[pl.ds(me * 6 + 3, 3)],
            send_sem=send_sem,
            recv_sem=landing((0, last)[side]),
            device_id=({"angle": 0, "row": after}, {"angle": last, "row": before})[side],
        )

    crossing = (cross_before, cross_after)
    outward = (cross_after, cross_before)

    def border_copies(side):
        target = (0, last)[side]

        @pl.when(crossing[side] & (me != target))
        def _():
            part_copy(side).start()

        @pl.when(jnp.logical_not(crossing[side]) & (me != target))
        def _():
            row_copy(target).start()

    def edge_start(side):
        @pl.when(outward[side])
        def _():
            edge_copy(side).start()

    reach = angles // GROUPS

    def tell(a):
        pl.semaphore_signal(ready.at[me // reach], inc=1, device_id={"angle": a})


    for p in range(PIECES):
        for b in range(p * PARTS, (p + 1) * PARTS) if rows > TILE else ():
            raw_copy(b, 0, 1).wait()
        loop(0, rows // TILE, lambda g: correlate(p, g))
        border(p, 0)
        rim(p, 0)

    pl.semaphore_wait(barrier, me + has_before.astype(jnp.int32) + has_after.astype(jnp.int32))

    @pl.when(even)
    def _():
        border_copies(0)
        halo_copy(0).start()

    @pl.when(odd)
    def _():
        edge_start(0)

    loop(0, me, tell)
    partner_copy.start()
    table_copy.start()
    for p in range(PIECES):
        loop(1, rows - 1, lambda i: interior(p, i))
        border(p, 1)
        rim(p, 1)

    @pl.when(odd)
    def _():
        halo_copy(1).start()

    def bulk():
        loop(1, jnp.minimum(me, last), lambda t: row_copy(t).start())

    @pl.when(even)
    def _():
        bulk()
        edge_start(1)

    @pl.when(odd)
    def _():
        halo_copy(0).wait_recv()
        joined(0)
        border_copies(0)
        bulk()

    @pl.when(even)
    def _():
        halo_copy(1).wait_recv()
        joined(1)

    for group in range(GROUPS):
        low, high = jnp.maximum(me + 1, group * reach), (group + 1) * reach

        @pl.when(low < high)
        def _():
            pl.semaphore_wait(ready.at[group], high - low)
            loop(low, min(high, last), lambda t: row_copy(t).start())

    border_copies(1)

    flat_copy.wait()
    for q in range(2):
        for c in range(chunks):
            flat_rows[q, c : c + 1, :] = steps * flat_ref[q : q + 1, c * LANES : (c + 1) * LANES].astype(jnp.float32)
    partner_copy.wait()
    table_copy.wait()

    @pl.when(jnp.logical_not(merged))
    def _():
        recv[me] = smooth[me]

    @pl.when(first_row)
    def _():
        both[pl.ds(me * 6, 3)] = partial[0]

    @pl.when(last_row)
    def _():
        both[pl.ds(me * 6, 3)] = partial[1]

    lane = lax.broadcasted_iota(jnp.int32, (TILE, LANES), 1)
    sublane = lax.broadcasted_iota(jnp.int32, (TILE, LANES), 0)
    middle = LANES // 2
    lower = lane < middle
    paired = 2 * jnp.where(lower, lane, lane - middle)
    odd_first = lower == (lax.rem(sublane, 2) == 0)
    onward = paired + odd_first.astype(jnp.int32)
    backward = LANES - 2 - paired + odd_first.astype(jnp.int32)

    def landed(at, units):
        pltpu.make_async_remote_copy(
            src_ref=both.at[pl.ds(0, units)], dst_ref=both.at[pl.ds(0, units)],
            send_sem=send_sem, recv_sem=recv_sem.at[at], device_id={"row": after},
        ).wait_recv()

    def merge(a):
        values = [both[a * 6 + q].astype(jnp.float32) + both[a * 6 + 3 + q].astype(jnp.float32) for q in range(3)]
        scale = 1.0 / values[2]
        for q in range(2):
            recv[a, q] = (values[q] * scale).astype(jnp.bfloat16)

    def differ(a):
        sine, cosine = recv[a, 1].astype(jnp.float32), recv[a, 0].astype(jnp.float32)
        value = sine * flat_rows[0] - cosine * flat_rows[1]
        dpc = value.astype(jnp.bfloat16).astype(jnp.float32)
        for c in range(0, chunks, TILE):
            natural[a, c : c + TILE, :] = jnp.take_along_axis(dpc[c : c + TILE], onward, axis=1)
            mirrored[a, c : c + TILE, :] = -jnp.take_along_axis(dpc[c : c + TILE], backward, axis=1)

    def others(body):
        loop(0, last, lambda k: body(lax.rem(final + 1 + k, angles)))

    @pl.when(merged)
    def _():
        landed(0, 6 * (angles - 2) + 3)
        others(merge)

    @pl.when(jnp.logical_not(merged))
    def _():
        landed(0, 2 * (angles - 2))

    others(differ)
    natural[final] = jnp.zeros(natural.shape[1:], natural.dtype)
    mirrored[final] = jnp.zeros(mirrored.shape[1:], mirrored.dtype)

    def turn(g):
        base = aligned(g * TILE, TILE)
        for c in range(0, chunks, TILE):
            here = jnp.swapaxes(jnp.stack([natural[base + j, c : c + TILE, :] for j in range(TILE)]), 0, 1)
            there = jnp.swapaxes(
                jnp.stack([mirrored[partner_ref[base + j], c : c + TILE, :] for j in range(TILE)]), 0, 1
            )
            for j in range(TILE):
                tiles[chunks + c + j, pl.ds(base, TILE), :] = here[j]
                tiles[chunks - 1 - c - j, pl.ds(base, TILE), :] = there[j]

    loop(0, angles // TILE, turn)

    @pl.when(merged)
    def _():
        landed(1, 6)
        merge(final)

    @pl.when(jnp.logical_not(merged))
    def _():
        landed(1, 2)

    differ(final)

    def place(g):
        base = aligned(g * TILE, TILE)
        here, there = sublane + base == final, sublane + base == partner_ref[final]

        def tile(c):
            if c < chunks:
                row = mirrored[final, chunks - 1 - c : chunks - c, :]
                return jnp.where(there, row, tiles[c, pl.ds(base, TILE), :])
            row = natural[final, c - chunks : c - chunks + 1, :]
            return jnp.where(here, row, tiles[c, pl.ds(base, TILE), :])

        uneven, turned = [], []
        for block in range(chunks):
            first, second = tile(2 * block), tile(2 * block + 1)
            uneven.append(jnp.where(lower, first, second))
            turned.append(pltpu.roll(jnp.where(lower, second, first), middle - 1, 1))
        for block in range(chunks):
            shifted = jnp.where(lane < LANES - 1, turned[block], turned[(block + 1) % chunks])
            group, half = divmod(block, 2)
            lanes = slice(half * LANES, (half + 1) * LANES)
            for k in (group, group + 2 * own)[: 2 if group < own else 1]:
                ring[pl.ds(2 * k * angles + base, TILE), lanes] = uneven[block]
                ring[pl.ds((2 * k + 1) * angles + base, TILE), lanes] = shifted

    loop(0, angles // TILE, place)

    turns = 2 * own
    height = 2 * own * angles
    total = jnp.zeros((height, WIDTH), jnp.float32)
    for m in range(turns):
        first = ((own - m) % turns) * 2 * angles
        window = ring[first : first + height].astype(jnp.bfloat16)
        total = total + jnp.dot(window, table[m], preferred_element_type=jnp.float32)
    total = total.astype(jnp.bfloat16).astype(jnp.float32)
    second_half = lane // 2 + middle
    for k in range(own):
        for half in range(2):
            lanes = slice(half * LANES, (half + 1) * LANES)
            for base in range(0, angles, TILE):
                at = 2 * k * angles + base
                even_at = total[at : at + TILE, lanes]
                odd_at = total[at + angles : at + angles + TILE, lanes]
                for part, index in enumerate((lane // 2, second_half)):
                    c = 4 * k + 2 * half + part
                    mixed = jnp.where(
                        lax.rem(lane, 2) == 0,
                        jnp.take_along_axis(even_at, index, axis=1),
                        jnp.take_along_axis(odd_at, index, axis=1),
                    )
                    out_ref[base : base + TILE, c * LANES : (c + 1) * LANES] = mixed.astype(jnp.bfloat16)

    crossed = cross_before | cross_after

    def sent(units):
        pltpu.make_async_remote_copy(
            src_ref=both.at[pl.ds(0, units)], dst_ref=both.at[pl.ds(0, units)],
            send_sem=send_sem, recv_sem=halo_sem, device_id={"row": after},
        ).wait_send()

    @pl.when(jnp.logical_not(crossed))
    def _():
        sent(2 * angles + 1)

    @pl.when(crossed & jnp.logical_not(merged))
    def _():
        sent(2 * angles + 5)

    @pl.when(merged)
    def _():
        sent(2 * angles + 4)


def local(raw_frames, step_index, partner, flat_field):
    _, steps, rows, det = raw_frames.shape
    angles = lax.axis_size("angle")
    blocks_row = lax.axis_size("row")
    chunks = det // LANES
    own = det // (2 * WIDTH)
    assert rows == angles and rows % TILE == 0 and blocks_row % 2 == 0 and angles % GROUPS == 0 and raw_frames.shape[0] == 1
    table = jnp.asarray(circulant_blocks(2 * det))

    def body(*refs):
        pl.run_scoped(
            lambda *own_sems: kernel(angles, blocks_row, *refs, *own_sems),
            pltpu.SemaphoreType.DMA((3 + PIECES * PARTS,)),
            pltpu.SemaphoreType.DMA,
        )

    result = pl.pallas_call(
        body,
        out_shape=jax.ShapeDtypeStruct((angles, det), jnp.bfloat16),
        in_specs=[pl.BlockSpec(memory_space=pltpu.HBM)] * 5,
        out_specs=pl.BlockSpec(memory_space=pltpu.VMEM),
        scratch_shapes=[
            *[pltpu.VMEM((steps, rows, det // (PIECES * PARTS)), jnp.bfloat16)] * (PIECES * PARTS),
            pltpu.VMEM(table.shape, jnp.bfloat16),
            pltpu.SMEM((1, steps), jnp.int32),
            pltpu.SMEM((angles,), jnp.int32),
            pltpu.VMEM((2, det), jnp.bfloat16),
            pltpu.VMEM((2, chunks, LANES), jnp.float32),
            pltpu.VMEM((3, rows * chunks, LANES), jnp.float32),
            pltpu.VMEM((3, chunks, LANES), jnp.bfloat16),
            pltpu.VMEM((2, 3, chunks, LANES), jnp.bfloat16),
            pltpu.VMEM((2, 3, chunks, LANES), jnp.bfloat16),
            pltpu.VMEM((angles * 6, chunks, LANES), jnp.bfloat16),
            pltpu.VMEM((rows, 2, chunks, LANES), jnp.bfloat16),
            pltpu.VMEM((angles, 2, chunks, LANES), jnp.bfloat16),
            pltpu.VMEM((angles, chunks, LANES), jnp.float32),
            pltpu.VMEM((angles, chunks, LANES), jnp.float32),
            pltpu.VMEM((2 * chunks, angles, LANES), jnp.float32),
            pltpu.VMEM((6 * own * angles, WIDTH), jnp.float32),
            pltpu.SemaphoreType.DMA,
            pltpu.SemaphoreType.DMA((2,)),
            pltpu.SemaphoreType.REGULAR((GROUPS,)),
        ],
        compiler_params=pltpu.CompilerParams(
            collective_id=0, has_side_effects=True, vmem_limit_bytes=48 * 1024 * 1024
        ),
    )(*[pltpu.with_memory_space_constraint(x, pltpu.HBM) for x in (raw_frames, step_index, partner, flat_field[:, 0, :], table)])
    return result[:, None, :]


def solution(mesh):
    in_specs = (
        P("angle", None, "row", None),
        P("angle", None),
        P(),
        P(None, ("row", "angle"), None),
    )
    out_specs = P(None, ("row", "angle"), None)
    return jax.shard_map(local, mesh=mesh, in_specs=in_specs, out_specs=out_specs, check_vma=False)
```

```python
import math

import jax
import jax.numpy as jnp
import ml_dtypes
import numpy as np
from jax import lax
from jax.experimental import pallas as pl
from jax.experimental.pallas import tpu as pltpu
from jax.sharding import PartitionSpec as P

WIDTH = 256
LANES = 128
TILE = 8
PIECES = 2
PARTS = 2
SPLIT = 2
GROUPS = 2


def circulant_blocks(padlen):
    count = padlen // (2 * WIDTH)
    n = np.arange(padlen, dtype=np.float64)
    odd = np.arange(padlen) % 2 == 1
    taps = np.where(odd, (2.0 / padlen) / np.tan(np.pi * np.where(odd, n, 1.0) / padlen), 0.0)
    m = np.arange(count)[:, None, None]
    p = np.arange(WIDTH)[None, :, None]
    q = np.arange(WIDTH)[None, None, :]
    return taps[(2 * (WIDTH * m + q - p) - 1) % padlen].astype(ml_dtypes.bfloat16)


def loop(start, stop, body):
    if isinstance(start, int) and isinstance(stop, int) and stop - start <= 8:
        for i in range(start, stop):
            body(i)
    else:
        lax.fori_loop(start, stop, lambda i, _: body(i), None)


def aligned(value, step):
    return value if isinstance(value, int) else pl.multiple_of(value, step)


def kernel(
    angles, blocks_row, raw_hbm, step_hbm, partner_hbm, flat_hbm, table_hbm, out_ref,
    raw_0, raw_1, raw_2, raw_3, table, step_ref, partner_ref, flat_ref, flat_rows, corr, halo, partial, edge, both, smooth, recv, natural, mirrored, tiles, ring,
    halo_sem, recv_sem, ready, local_sem, send_sem,
):
    raw = (raw_0, raw_1, raw_2, raw_3)
    steps, rows, _ = raw_0.shape
    det = flat_ref.shape[1]
    chunks = det // LANES
    per = chunks // PIECES
    own = det // (2 * WIDTH)
    last = angles - 1
    me = lax.axis_index("angle")
    row = lax.axis_index("row")
    after = lax.rem(row + 1, blocks_row)
    before = lax.rem(row + blocks_row - 1, blocks_row)
    has_before = row > 0
    has_after = row < blocks_row - 1
    odd = lax.rem(row, 2) == 1
    even = jnp.logical_not(odd)
    cross_before = has_before & even
    cross_after = has_after & odd
    first_row = (me == 0) & cross_before
    last_row = (me == last) & cross_after
    merged = first_row | last_row

    final = jnp.where(me < angles // 2, last, 0)

    def landing(target):
        other = jnp.where(target < angles // 2, last, 0)
        return recv_sem.at[(me == other).astype(jnp.int32)]

    barrier = pltpu.get_barrier_semaphore()

    step_copy = pltpu.make_async_copy(step_hbm, step_ref, local_sem.at[0])
    step_copy.start()

    def raw_copy(b, part, parts):
        width = raw_0.shape[2] // parts
        return pltpu.make_async_copy(
            raw_hbm.at[0, :, :, pl.ds(b * raw_0.shape[2] + part * width, width)],
            raw[b].at[:, :, pl.ds(part * width, width)],
            local_sem.at[3 + b],
        )

    for b in range(PIECES * PARTS):
        for part in range(SPLIT):
            raw_copy(b, part, SPLIT).start()

    def greet(a):
        pl.semaphore_signal(barrier, inc=1, device_id={"angle": a})

    loop(0, last - me, lambda k: greet(last - k))

    @pl.when(even)
    def _():
        pl.semaphore_signal(barrier, inc=1, device_id={"row": after})

    @pl.when(odd)
    def _():
        pl.semaphore_signal(barrier, inc=1, device_id={"row": before})

    @pl.when(first_row)
    def _():
        loop(0, angles, lambda a: pl.semaphore_signal(
            barrier, inc=1, device_id={"angle": a, "row": before}
        ))

    @pl.when(last_row)
    def _():
        loop(0, angles, lambda a: pl.semaphore_signal(
            barrier, inc=1, device_id={"angle": a, "row": after}
        ))

    step_copy.wait()
    flat_copy = pltpu.make_async_copy(flat_hbm, flat_ref, local_sem.at[0])
    flat_copy.start()
    partner_copy = pltpu.make_async_copy(partner_hbm, partner_ref, local_sem.at[1])
    table_copy = pltpu.make_async_copy(table_hbm, table, local_sem.at[2])

    named = [step_ref[0, k] for k in range(steps)]
    frame_of = []
    for i in range(steps):
        at = jnp.int32(0)
        for k in range(1, steps):
            at = jnp.where(named[k] == i, jnp.int32(k), at)
        frame_of.append(at)
    assert steps == 8
    half_root = float(np.float32(math.sqrt(0.5)))

    def correlate(p, g):
        at = aligned(g * TILE, TILE)
        sums = [[], [], []]
        for c in range(per):
            b, c = p * PARTS + c // (per // PARTS), c % (per // PARTS)
            if rows == TILE and c == 0:
                raw_copy(b, 0, 1).wait()
            f = [
                raw[b][frame_of[i], pl.ds(at, TILE), c * LANES : (c + 1) * LANES].astype(jnp.float32)
                for i in range(steps)
            ]
            less = [f[i] - f[i + 4] for i in range(4)]
            more = [f[i] + f[i + 4] for i in range(4)]
            sums[0].append(less[0] + (less[1] - less[3]) * half_root)
            sums[1].append(less[2] + (less[1] + less[3]) * half_root)
            sums[2].append((more[0] + more[2]) + (more[1] + more[3]))
        for q in range(3):
            turned = jnp.swapaxes(jnp.stack(sums[q]), 0, 1)
            for j in range(TILE):
                corr[q, pl.ds(aligned((at + j) * chunks + p * per, TILE), per), :] = turned[j]

    def line(p, q, i):
        return corr[q, pl.ds(aligned(i * chunks + p * per, TILE), per), :]

    def part_of(p):
        return slice(p * per, (p + 1) * per)

    def ratios(p, i, values):
        values = [v.astype(jnp.bfloat16).astype(jnp.float32) for v in values]
        scale = 1.0 / values[2]
        for q in range(2):
            smooth[i, q, part_of(p), :] = (values[q] * scale).astype(jnp.bfloat16)

    def interior(p, i):
        ratios(p, i, [
            0.25 * line(p, q, i - 1) + 0.5 * line(p, q, i) + 0.25 * line(p, q, i + 1) for q in range(3)
        ])

    def border(p, side):
        at, inside = ((0, 1), (rows - 1, rows - 2))[side]
        inner = [0.5 * line(p, q, at) + 0.25 * line(p, q, inside) for q in range(3)]
        for q in range(3):
            partial[side, q, part_of(p), :] = inner[q].astype(jnp.bfloat16)
        ratios(p, at, inner)

    def rim(p, side):
        for q in range(3):
            edge[side, q, part_of(p), :] = (0.25 * line(p, q, (rows - 1, 0)[side])).astype(jnp.bfloat16)

    def joined(side):
        at, inside = ((0, 1), (rows - 1, rows - 2))[side]
        for p in range(PIECES):
            ratios(p, at, [
                halo[q, part_of(p), :].astype(jnp.float32) + 0.5 * line(p, q, at) + 0.25 * line(p, q, inside)
                for q in range(3)
            ])

    def halo_copy(side):
        return pltpu.make_async_remote_copy(
            src_ref=edge.at[side],
            dst_ref=halo,
            send_sem=send_sem,
            recv_sem=halo_sem,
            device_id={"row": (after, before)[side]},
        )

    def row_copy(target):
        return pltpu.make_async_remote_copy(
            src_ref=smooth.at[target],
            dst_ref=recv.at[me],
            send_sem=send_sem,
            recv_sem=landing(target),
            device_id={"angle": target},
        )

    def part_copy(side):
        return pltpu.make_async_remote_copy(
            src_ref=partial.at[side],
            dst_ref=both.at[pl.ds(me * 6, 3)],
            send_sem=send_sem,
            recv_sem=landing((0, last)[side]),
            device_id={"angle": (0, last)[side]},
        )

    def edge_copy(side):
        return pltpu.make_async_remote_copy(
            src_ref=edge.at[side],
            dst_ref=both.at[pl.ds(me * 6 + 3, 3)],
            send_sem=send_sem,
            recv_sem=landing((0, last)[side]),
            device_id=({"angle": 0, "row": after}, {"angle": last, "row": before})[side],
        )

    crossing = (cross_before, cross_after)
    outward = (cross_after, cross_before)

    def border_copies(side):
        target = (0, last)[side]

        @pl.when(crossing[side] & (me != target))
        def _():
            part_copy(side).start()

        @pl.when(jnp.logical_not(crossing[side]) & (me != target))
        def _():
            row_copy(target).start()

    def edge_start(side):
        @pl.when(outward[side])
        def _():
            edge_copy(side).start()

    reach = angles // GROUPS

    def tell(a):
        pl.semaphore_signal(ready.at[me // reach], inc=1, device_id={"angle": a})


    for p in range(PIECES):
        for b in range(p * PARTS, (p + 1) * PARTS) if rows > TILE else ():
            raw_copy(b, 0, 1).wait()
        loop(0, rows // TILE, lambda g: correlate(p, g))
        border(p, 0)
        rim(p, 0)

    pl.semaphore_wait(barrier, me + has_before.astype(jnp.int32) + has_after.astype(jnp.int32))

    @pl.when(even)
    def _():
        border_copies(0)
        halo_copy(0).start()

    @pl.when(odd)
    def _():
        edge_start(0)

    loop(0, me, tell)
    partner_copy.start()
    table_copy.start()
    for p in range(PIECES):
        loop(1, rows - 1, lambda i: interior(p, i))
        border(p, 1)
        rim(p, 1)

    @pl.when(odd)
    def _():
        halo_copy(1).start()

    def bulk():
        loop(1, jnp.minimum(me, last), lambda t: row_copy(t).start())

    @pl.when(even)
    def _():
        bulk()
        edge_start(1)

    @pl.when(odd)
    def _():
        halo_copy(0).wait_recv()
        joined(0)
        border_copies(0)
        bulk()

    @pl.when(even)
    def _():
        halo_copy(1).wait_recv()
        joined(1)

    for group in range(GROUPS):
        low, high = jnp.maximum(me + 1, group * reach), (group + 1) * reach

        @pl.when(low < high)
        def _():
            pl.semaphore_wait(ready.at[group], high - low)
            loop(low, min(high, last), lambda t: row_copy(t).start())

    border_copies(1)

    flat_copy.wait()
    for q in range(2):
        for c in range(chunks):
            flat_rows[q, c : c + 1, :] = steps * flat_ref[q : q + 1, c * LANES : (c + 1) * LANES].astype(jnp.float32)
    partner_copy.wait()
    table_copy.wait()

    @pl.when(jnp.logical_not(merged))
    def _():
        recv[me] = smooth[me]

    @pl.when(first_row)
    def _():
        both[pl.ds(me * 6, 3)] = partial[0]

    @pl.when(last_row)
    def _():
        both[pl.ds(me * 6, 3)] = partial[1]

    lane = lax.broadcasted_iota(jnp.int32, (TILE, LANES), 1)
    sublane = lax.broadcasted_iota(jnp.int32, (TILE, LANES), 0)
    middle = LANES // 2
    lower = lane < middle
    paired = 2 * jnp.where(lower, lane, lane - middle)
    odd_first = lower == (lax.rem(sublane, 2) == 0)
    onward = paired + odd_first.astype(jnp.int32)
    backward = LANES - 2 - paired + odd_first.astype(jnp.int32)

    def landed(at, units):
        pltpu.make_async_remote_copy(
            src_ref=both.at[pl.ds(0, units)], dst_ref=both.at[pl.ds(0, units)],
            send_sem=send_sem, recv_sem=recv_sem.at[at], device_id={"row": after},
        ).wait_recv()

    def merge(a):
        values = [both[a * 6 + q].astype(jnp.float32) + both[a * 6 + 3 + q].astype(jnp.float32) for q in range(3)]
        scale = 1.0 / values[2]
        for q in range(2):
            recv[a, q] = (values[q] * scale).astype(jnp.bfloat16)

    def differ(a):
        sine, cosine = recv[a, 1].astype(jnp.float32), recv[a, 0].astype(jnp.float32)
        value = sine * flat_rows[0] - cosine * flat_rows[1]
        dpc = value.astype(jnp.bfloat16).astype(jnp.float32)
        for c in range(0, chunks, TILE):
            natural[a, c : c + TILE, :] = jnp.take_along_axis(dpc[c : c + TILE], onward, axis=1)
            mirrored[a, c : c + TILE, :] = -jnp.take_along_axis(dpc[c : c + TILE], backward, axis=1)

    def others(body):
        loop(0, last, lambda k: body(lax.rem(final + 1 + k, angles)))

    @pl.when(merged)
    def _():
        landed(0, 6 * (angles - 2) + 3)
        others(merge)

    @pl.when(jnp.logical_not(merged))
    def _():
        landed(0, 2 * (angles - 2))

    others(differ)
    natural[final] = jnp.zeros(natural.shape[1:], natural.dtype)
    mirrored[final] = jnp.zeros(mirrored.shape[1:], mirrored.dtype)

    def turn(g):
        base = aligned(g * TILE, TILE)
        for c in range(0, chunks, TILE):
            here = jnp.swapaxes(jnp.stack([natural[base + j, c : c + TILE, :] for j in range(TILE)]), 0, 1)
            there = jnp.swapaxes(
                jnp.stack([mirrored[partner_ref[base + j], c : c + TILE, :] for j in range(TILE)]), 0, 1
            )
            for j in range(TILE):
                tiles[chunks + c + j, pl.ds(base, TILE), :] = here[j]
                tiles[chunks - 1 - c - j, pl.ds(base, TILE), :] = there[j]

    loop(0, angles // TILE, turn)

    @pl.when(merged)
    def _():
        landed(1, 6)
        merge(final)

    @pl.when(jnp.logical_not(merged))
    def _():
        landed(1, 2)

    differ(final)

    def place(g):
        base = aligned(g * TILE, TILE)
        here, there = sublane + base == final, sublane + base == partner_ref[final]

        def tile(c):
            if c < chunks:
                row = mirrored[final, chunks - 1 - c : chunks - c, :]
                return jnp.where(there, row, tiles[c, pl.ds(base, TILE), :])
            row = natural[final, c - chunks : c - chunks + 1, :]
            return jnp.where(here, row, tiles[c, pl.ds(base, TILE), :])

        uneven, turned = [], []
        for block in range(chunks):
            first, second = tile(2 * block), tile(2 * block + 1)
            uneven.append(jnp.where(lower, first, second))
            turned.append(pltpu.roll(jnp.where(lower, second, first), middle - 1, 1))
        for block in range(chunks):
            shifted = jnp.where(lane < LANES - 1, turned[block], turned[(block + 1) % chunks])
            group, half = divmod(block, 2)
            lanes = slice(half * LANES, (half + 1) * LANES)
            for k in (group, group + 2 * own)[: 2 if group < own else 1]:
                ring[pl.ds(2 * k * angles + base, TILE), lanes] = uneven[block].astype(jnp.bfloat16)
                ring[pl.ds((2 * k + 1) * angles + base, TILE), lanes] = shifted.astype(jnp.bfloat16)

    loop(0, angles // TILE, place)

    turns = 2 * own
    height = 2 * own * angles
    total = jnp.zeros((height, WIDTH), jnp.float32)
    for m in range(turns):
        first = ((own - m) % turns) * 2 * angles
        window = ring[first : first + height]
        total = total + jnp.dot(window, table[m], preferred_element_type=jnp.float32)
    total = total.astype(jnp.bfloat16).astype(jnp.float32)
    second_half = lane // 2 + middle
    for k in range(own):
        for half in range(2):
            lanes = slice(half * LANES, (half + 1) * LANES)
            for base in range(0, angles, TILE):
                at = 2 * k * angles + base
                even_at = total[at : at + TILE, lanes]
                odd_at = total[at + angles : at + angles + TILE, lanes]
                for part, index in enumerate((lane // 2, second_half)):
                    c = 4 * k + 2 * half + part
                    mixed = jnp.where(
                        lax.rem(lane, 2) == 0,
                        jnp.take_along_axis(even_at, index, axis=1),
                        jnp.take_along_axis(odd_at, index, axis=1),
                    )
                    out_ref[base : base + TILE, c * LANES : (c + 1) * LANES] = mixed.astype(jnp.bfloat16)

    crossed = cross_before | cross_after

    def sent(units):
        pltpu.make_async_remote_copy(
            src_ref=both.at[pl.ds(0, units)], dst_ref=both.at[pl.ds(0, units)],
            send_sem=send_sem, recv_sem=halo_sem, device_id={"row": after},
        ).wait_send()

    @pl.when(jnp.logical_not(crossed))
    def _():
        sent(2 * angles + 1)

    @pl.when(crossed & jnp.logical_not(merged))
    def _():
        sent(2 * angles + 5)

    @pl.when(merged)
    def _():
        sent(2 * angles + 4)


def local(raw_frames, step_index, partner, flat_field):
    _, steps, rows, det = raw_frames.shape
    angles = lax.axis_size("angle")
    blocks_row = lax.axis_size("row")
    chunks = det // LANES
    own = det // (2 * WIDTH)
    assert rows == angles and rows % TILE == 0 and blocks_row % 2 == 0 and angles % GROUPS == 0 and raw_frames.shape[0] == 1
    table = jnp.asarray(circulant_blocks(2 * det))

    def body(*refs):
        pl.run_scoped(
            lambda *own_sems: kernel(angles, blocks_row, *refs, *own_sems),
            pltpu.SemaphoreType.DMA((3 + PIECES * PARTS,)),
            pltpu.SemaphoreType.DMA,
        )

    result = pl.pallas_call(
        body,
        out_shape=jax.ShapeDtypeStruct((angles, det), jnp.bfloat16),
        in_specs=[pl.BlockSpec(memory_space=pltpu.HBM)] * 5,
        out_specs=pl.BlockSpec(memory_space=pltpu.VMEM),
        scratch_shapes=[
            *[pltpu.VMEM((steps, rows, det // (PIECES * PARTS)), jnp.bfloat16)] * (PIECES * PARTS),
            pltpu.VMEM(table.shape, jnp.bfloat16),
            pltpu.SMEM((1, steps), jnp.int32),
            pltpu.SMEM((angles,), jnp.int32),
            pltpu.VMEM((2, det), jnp.bfloat16),
            pltpu.VMEM((2, chunks, LANES), jnp.float32),
            pltpu.VMEM((3, rows * chunks, LANES), jnp.float32),
            pltpu.VMEM((3, chunks, LANES), jnp.bfloat16),
            pltpu.VMEM((2, 3, chunks, LANES), jnp.bfloat16),
            pltpu.VMEM((2, 3, chunks, LANES), jnp.bfloat16),
            pltpu.VMEM((angles * 6, chunks, LANES), jnp.bfloat16),
            pltpu.VMEM((rows, 2, chunks, LANES), jnp.bfloat16),
            pltpu.VMEM((angles, 2, chunks, LANES), jnp.bfloat16),
            pltpu.VMEM((angles, chunks, LANES), jnp.float32),
            pltpu.VMEM((angles, chunks, LANES), jnp.float32),
            pltpu.VMEM((2 * chunks, angles, LANES), jnp.float32),
            pltpu.VMEM((6 * own * angles, WIDTH), jnp.bfloat16),
            pltpu.SemaphoreType.DMA,
            pltpu.SemaphoreType.DMA((2,)),
            pltpu.SemaphoreType.REGULAR((GROUPS,)),
        ],
        compiler_params=pltpu.CompilerParams(
            collective_id=0, has_side_effects=True, vmem_limit_bytes=48 * 1024 * 1024
        ),
    )(*[pltpu.with_memory_space_constraint(x, pltpu.HBM) for x in (raw_frames, step_index, partner, flat_field[:, 0, :], table)])
    return result[:, None, :]


def solution(mesh):
    in_specs = (
        P("angle", None, "row", None),
        P("angle", None),
        P(),
        P(None, ("row", "angle"), None),
    )
    out_specs = P(None, ("row", "angle"), None)
    return jax.shard_map(local, mesh=mesh, in_specs=in_specs, out_specs=out_specs, check_vma=False)
```
